256 devices in a mesh: gx: 8 (over y, core), gy: 8 (over x, z_lo), gz: 4 (over z_hi).
Axes of the slice: x: 4, y: 4, z: 8 (z_hi: 4, z_lo: 2; z = z_hi * 2 + z_lo), core: 2. Of those that a mesh axis runs over, the one named last changes fastest.
Arguments:
- rhs: float32 [8, 8, 3, 162, 1024], P('gx', 'gy', None, None, 'gz'), may hold values from -6 to 6
- angles: float32 [8, 8, 3, 1024], P('gx', 'gy', None, 'gz'), may hold values from -3.140625 to 3.140625
- self_mob: float32 [486, 486], replicated, may hold values from -0.25 to 0.25
- near_mat: float32 [486, 486], replicated, may hold values from -0.25 to 0.25
- near_weight: float32 [8, 8, 8, 1024], P('gx', 'gy', None, 'gz'), may hold values from -2 to 2
- neighbours: int32 [8, 8, 8, 1024], P('gx', 'gy', None, 'gz'), may hold values from 0 to 2111, as said below
- cells: int32 [8, 8, 1024], P('gx', 'gy', 'gz'), may hold values from 0 to 191
- blob_weight: float32 [162], replicated, may hold values from -0.5 to 0.5
- skel_perm: int32 [2, 384], replicated, may hold values from 0 to 383, each once within a row
- interp: float32 [2, 192, 192], replicated, may hold values from -0.4375 to 0.4375
- sibling_ops: float32 [2, 192, 192], replicated, may hold values from -0.375 to 0.375
- root_op: float32 [192, 192], replicated, may hold values from -0.0625 to 0.0625
Outputs:
- solution: float32 [8, 8, 3, 162, 1024], P('gx', 'gy', None, None, 'gz')
- lsq_residual: float32 [], replicated
The draws below stay inside these ranges and needn't reach their ends.
Inputs may be any that keep to these rules, and one draw needn't show every extreme that they name: `neighbours`: each id is s * 256 + j with slot s in 0..8 and j < 256; j < 64 whenever s != 4, and some id in every draw reaches j = 63 in slot 8.
All inputs are finite; a program needn't handle non-finite values.
Results may differ from the reference program's by a relative error of at most 0.0003.
Values sent between devices are 32-bit elements; how exact they have to be, the bound alone decides.
A program may use at most 128 MiB of HBM per device.

```python
import jax
import jax.numpy as jnp
from jax import lax

BLOBS = 162
SKEL = 192
NEIGH = 8
LEVELS = 2
B_DEV = 256
DOF = 486
RIM = 64
COLS = 1024
N_GX = 8
N_GY = 8
N_GZ = 4


def draw_neighbours(key, part):
    key_slot, key_own, key_rim = jax.random.split(key, 3)
    shape = (N_GX, N_GY, NEIGH, COLS)
    box_slot = jax.random.randint(key_slot, shape, 0, 9)
    own_body = jax.random.randint(key_own, shape, 0, B_DEV)
    rim_body = jax.random.randint(key_rim, shape, 0, RIM)
    ids = jnp.where(box_slot == 4, box_slot * B_DEV + own_body, box_slot * B_DEV + rim_body)
    ids = ids.at[0, 0, 0, 0].set(0)
    ids = ids.at[0, 0, 1, 0].set(8 * B_DEV + RIM - 1)
    return ids.astype(jnp.int32)


def set_ends(entries, stream_key, least, top_value):
    extent = entries.shape
    index_at = [jax.random.randint(jax.random.fold_in(stream_key, axis), (), 0, extent[axis]) for axis in range(len(extent))]
    entries = entries.at[tuple(index_at)].set(least)
    longest = extent.index(max(extent))
    index_at[longest] = (index_at[longest] + 1) % extent[longest]
    return entries.at[tuple(index_at)].set(top_value)


def steps_of(own_key, extent, cuts, smallest, high):
    factor_of = 1.0
    for position, shards_of in cuts:
        heights = jax.random.uniform(jax.random.fold_in(jax.random.fold_in(own_key, 6), position), (shards_of,), jnp.float32, smallest / len(cuts), high / len(cuts))
        factor_of = factor_of * jnp.repeat(jnp.exp(heights), extent[position] // shards_of).reshape((-1,) + (1,) * (len(extent) - 1 - position))
    return factor_of


def bell_draw(own_key, extent, width, most, pieces=(), kind=jnp.bfloat16):
    drawn = width * jax.random.normal(own_key, extent, jnp.float32)
    if pieces:
        drawn = drawn * steps_of(own_key, extent, pieces, -0.22, 0.18)
    return jnp.clip(drawn, -most, most).astype(kind)


def setup_inputs(seed: int = 0) -> dict:
    seeds = jax.random.split(jax.random.key(seed), 13)
    return {
        "rhs": bell_draw(seeds[0], (N_GX, N_GY, 3, BLOBS, COLS), 1.0, 6.0, ((0, 8), (1, 8), (4, 4)), jnp.float32),
        "angles": jnp.clip(jax.random.uniform(seeds[1], (N_GX, N_GY, 3, COLS), jnp.float32, -3.140625, 3.140625), -3.140625, 3.140625),
        "self_mob": bell_draw(seeds[2], (DOF, DOF), DOF ** -0.5, 0.25, (), jnp.float32),
        "near_mat": bell_draw(seeds[3], (DOF, DOF), DOF ** -0.5, 0.25, (), jnp.float32),
        "near_weight": bell_draw(seeds[4], (N_GX, N_GY, NEIGH, COLS), 0.35, 2.0, ((0, 8), (1, 8), (3, 4)), jnp.float32),
        "neighbours": draw_neighbours(jax.random.fold_in(seeds[12], 71), 0),
        "cells": set_ends(jax.random.randint(seeds[6], (N_GX, N_GY, COLS), 0, SKEL), jax.random.fold_in(seeds[6], 1), 0, SKEL - 1).astype(jnp.int32),
        "blob_weight": bell_draw(seeds[7], (BLOBS,), BLOBS ** -0.5, 0.5, (), jnp.float32),
        "skel_perm": jax.vmap(lambda own: jax.random.permutation(own, 2 * SKEL))(jax.random.split(seeds[8], LEVELS)).reshape((LEVELS, 2 * SKEL)).astype(jnp.int32),
        "interp": bell_draw(seeds[9], (LEVELS, SKEL, SKEL), SKEL ** -0.5, 0.4375, (), jnp.float32),
        "sibling_ops": bell_draw(seeds[10], (LEVELS, SKEL, SKEL), 0.06, 0.375, (), jnp.float32),
        "root_op": bell_draw(seeds[11], (SKEL, SKEL), 0.01, 0.0625, (), jnp.float32),
    }


highest = lax.Precision.HIGHEST
epsilon = 1e-06

def frame(angles):
    cos_yaw = jnp.cos(angles[0])
    sin_yaw = jnp.sin(angles[0])
    cos_pitch = jnp.cos(angles[1])
    sin_pitch = jnp.sin(angles[1])
    cos_roll = jnp.cos(angles[2])
    sin_roll = jnp.sin(angles[2])
    return ((cos_yaw * cos_pitch, cos_yaw * sin_pitch * sin_roll - sin_yaw * cos_roll, cos_yaw * sin_pitch * cos_roll + sin_yaw * sin_roll), (sin_yaw * cos_pitch, sin_yaw * sin_pitch * sin_roll + cos_yaw * cos_roll, sin_yaw * sin_pitch * cos_roll - cos_yaw * sin_roll), (-sin_pitch, cos_pitch * sin_roll, cos_pitch * cos_roll))

def rotate(source, rotation, inverse):
    components = []
    for target_axis in range(3):
        summed = jnp.zeros_like(source[0])
        for source_axis in range(3):
            factor = rotation[source_axis][target_axis] if inverse else rotation[target_axis][source_axis]
            summed = summed + factor[None, :] * source[source_axis]
        components.append(summed)
    return jnp.stack(components)

def least_squares(beta, diag_first, below_first, above_second, diag_second, below_second):
    first_norm = jnp.sqrt(diag_first * diag_first + below_first * below_first)
    first_cos = diag_first / first_norm
    first_sin = below_first / first_norm
    top_right = first_cos * above_second + first_sin * diag_second
    lower_right = first_cos * diag_second - first_sin * above_second
    second_norm = jnp.sqrt(lower_right * lower_right + below_second * below_second)
    second_cos = lower_right / second_norm
    second_sin = below_second / second_norm
    carried = -first_sin * beta
    coef_two = second_cos * carried / second_norm
    coef_one = (first_cos * beta - top_right * coef_two) / first_norm
    return (coef_one, coef_two, jnp.abs(second_sin * carried))

def reference(rhs, angles, self_mob, near_mat, near_weight, neighbours, cells, blob_weight, skel_perm, interp, sibling_ops, root_op):
    vector = jnp.transpose(rhs, (2, 3, 0, 1, 4)).reshape(3, BLOBS, -1)
    rotation = frame(jnp.transpose(angles, (2, 0, 1, 3)).reshape(3, -1))
    coef = jnp.transpose(near_weight, (2, 0, 1, 3)).reshape(NEIGH, -1)
    box_x = jnp.arange(N_GX, dtype=jnp.int32)[:, None, None, None]
    box_y = jnp.arange(N_GY, dtype=jnp.int32)[None, :, None, None]
    column = jnp.arange(COLS, dtype=jnp.int32)[None, None, None, :]
    box_slot = neighbours // B_DEV
    body_slot = neighbours % B_DEV
    target_x = (box_x + box_slot // 3 - 1) % N_GX
    target_y = (box_y + box_slot % 3 - 1) % N_GY
    target = (target_x * N_GY + target_y) * COLS + column // B_DEV * B_DEV + body_slot
    global_ids = jnp.transpose(target, (2, 0, 1, 3)).reshape(NEIGH, -1).astype(jnp.int32)
    leaf_cells = cells.reshape(N_GX, N_GY, N_GZ, B_DEV)
    occupancy = (leaf_cells[..., None] == jnp.arange(SKEL, dtype=jnp.int32)).astype(jnp.float32)
    layers = jnp.arange(N_GZ, dtype=jnp.int32)

    def operate(source):
        turned = rotate(source, rotation, False).reshape(DOF, -1)
        mixture = jnp.dot(self_mob, turned, precision=highest).reshape(3, BLOBS, -1)
        own_part = source + rotate(mixture, rotation, True)
        flat = source.reshape(DOF, -1)
        gathered = jnp.zeros_like(flat)
        for link_index in range(NEIGH):
            gathered = gathered + coef[link_index][None, :] * jnp.take(flat, global_ids[link_index], axis=1)
        near_part = jnp.dot(near_mat, gathered, precision=highest).reshape(3, BLOBS, -1)
        moments = jnp.einsum('cqn,q->cn', source, blob_weight, precision=highest)
        moments = moments.reshape(3, N_GX, N_GY, N_GZ, B_DEV)
        charges = jnp.einsum('cxyzb,xyzbj->xyzcj', moments, occupancy, precision=highest)
        partners = []
        high_flags = []
        for tree_level in range(LEVELS):
            partner = charges[:, :, layers ^ 1 << tree_level]
            high_side = (layers >> tree_level & 1 == 1)[None, None, :, None, None]
            low_child = jnp.where(high_side, partner, charges)
            higher = jnp.where(high_side, charges, partner)
            joined = jnp.concatenate([low_child, higher], axis=-1)
            picked = joined[..., skel_perm[tree_level]]
            charges = picked[..., :SKEL] + jnp.einsum('xyzcj,jk->xyzck', picked[..., SKEL:], interp[tree_level], precision=highest)
            partners.append(partner)
            high_flags.append(high_side)
        root_total = lax.optimization_barrier(jnp.sum(charges, axis=(0, 1), keepdims=True))
        potential = jnp.einsum('xyzcj,jk->xyzck', root_total - charges, root_op, precision=highest)
        for tree_level in reversed(range(LEVELS)):
            extra = jnp.einsum('xyzcj,kj->xyzck', potential, interp[tree_level], precision=highest)
            spread = jnp.concatenate([potential, extra], axis=-1)
            placed = jnp.zeros_like(spread).at[..., skel_perm[tree_level]].set(spread)
            child_part = jnp.where(high_flags[tree_level], placed[..., SKEL:], placed[..., :SKEL])
            potential = child_part + jnp.einsum('xyzcj,jk->xyzck', partners[tree_level], sibling_ops[tree_level], precision=highest)
        body_values = jnp.einsum('xyzcj,xyzbj->cxyzb', potential, occupancy, precision=highest).reshape(3, -1)
        far_part = blob_weight[None, :, None] * body_values[:, None, :]
        return own_part + near_part + far_part
    beta = jnp.sqrt(jnp.sum(vector * vector) + epsilon)
    basis_one = vector / beta
    image_one = operate(basis_one)
    diag_first = jnp.sum(image_one * basis_one)
    residue_one = image_one - diag_first * basis_one
    below_first = jnp.sqrt(jnp.sum(residue_one * residue_one) + epsilon)
    basis_two = residue_one / below_first
    image_two = operate(basis_two)
    above_second = jnp.sum(image_two * basis_one)
    diag_second = jnp.sum(image_two * basis_two)
    residue_two = image_two - above_second * basis_one - diag_second * basis_two
    below_second = jnp.sqrt(jnp.sum(residue_two * residue_two) + epsilon)
    coef_one, coef_two, lsq_residual = least_squares(beta, diag_first, below_first, above_second, diag_second, below_second)
    result = coef_one * basis_one + coef_two * basis_two
    solution = jnp.transpose(result.reshape(3, BLOBS, N_GX, N_GY, COLS), (2, 3, 0, 1, 4))
    return (solution, lsq_residual)
```

```python
import jax
import jax.numpy as jnp
from jax import lax
from jax.experimental import pallas as pl
from jax.experimental.pallas import tpu as pltpu
from jax.sharding import PartitionSpec as P

F32 = jnp.float32
BF16 = jnp.bfloat16
MESH = pl.DeviceIdType.MESH
epsilon = 1e-06

BLOBS = 162
PITCH = 168
ROWS = 512
BODIES = 256
SKEL = 192
CELLS = 256
RIM = 64
NEIGH = 8
NN = (((1,), (0,)), ((), ()))
NT = (((1,), (1,)), ((), ()))
OFFSETS = [(-1, -1), (-1, 0), (-1, 1), (0, -1), (0, 1), (1, -1), (1, 0), (1, 1)]
PLACE = {offset: index for index, offset in enumerate(OFFSETS)}


def split(x):
    high = x.astype(BF16)
    return high, (x - high.astype(F32)).astype(BF16)


def mm(a, b, dims=NN):
    return lax.dot_general(a, b, dims, preferred_element_type=F32)


def mm3(a, b, dims=NN):
    return mm(a[0], b[0], dims) + (mm(a[0], b[1], dims) + mm(a[1], b[0], dims))


def stacked(x):
    high = x.astype(BF16).astype(F32)
    return jnp.concatenate([high, x - high], axis=0).astype(BF16)


def fold(x):
    half = x.shape[0] // 2
    return x[:half] + x[half:]


def mm_few(x, weights, dims=NN):
    both = stacked(x)
    return fold(mm(both, weights[0], dims) + mm(both, weights[1], dims))


def total(x):
    return jnp.sum(x, axis=(0, 1), keepdims=True)


def iota(shape, dim):
    return lax.broadcasted_iota(jnp.int32, shape, dim)


def frame(angles):
    cos_all, sin_all = jnp.cos(angles), jnp.sin(angles)
    cy, cp, cr = cos_all[0:1], cos_all[1:2], cos_all[2:3]
    sy, sp, sr = sin_all[0:1], sin_all[1:2], sin_all[2:3]
    return (
        (cy * cp, cy * sp * sr - sy * cr, cy * sp * cr + sy * sr),
        (sy * cp, sy * sp * sr + cy * cr, sy * sp * cr - cy * sr),
        (-sp, cp * sr, cp * cr),
    )


def least_squares(beta, diag_first, below_first, above_second, diag_second, below_second):
    first_norm = jnp.sqrt(diag_first * diag_first + below_first * below_first)
    first_cos = diag_first / first_norm
    first_sin = below_first / first_norm
    top_right = first_cos * above_second + first_sin * diag_second
    lower_right = first_cos * diag_second - first_sin * above_second
    second_norm = jnp.sqrt(lower_right * lower_right + below_second * below_second)
    second_cos = lower_right / second_norm
    second_sin = below_second / second_norm
    carried = -first_sin * beta
    coef_two = second_cos * carried / second_norm
    coef_one = (first_cos * beta - top_right * coef_two) / first_norm
    return (coef_one, coef_two, jnp.abs(second_sin * carried))


def kernel(
    sizes,
    rhs_hbm, angles_hbm, self_hbm, near_hbm, weight_hbm, links_hbm, cells_hbm, blob_hbm, perm_hbm, interp_hbm, sibling_hbm, root_hbm,
    u_hbm, coef_ref,
    rhs_in, angles_in, self_in, near_in, weight_in, links_in, cells_in, blob_in, perm_in, interp_in, sibling_in, root_in,
    state_r, state_u, state_t, padded_mat, self_op, near_op, link_op, link_cols, link_rows, occupancy, blob_row, blob_col, rotation,
    perm_row, square, up_op, sibling_op, root_op, own_gather, u_out,
    rim, halo, stage_x, stage_y, stage_z,
    in_sem, out_sem, rim_send, rim_recv, x_send, x_recv, y_send, y_recv, z_send, z_recv,
):
    nx, ny, nz = sizes
    ix, iy, iz = lax.axis_index("gx"), lax.axis_index("gy"), lax.axis_index("gz")
    pending = []

    hbm = [rhs_hbm, blob_hbm, cells_hbm, angles_hbm, self_hbm, near_hbm, weight_hbm, links_hbm, perm_hbm, interp_hbm, sibling_hbm, root_hbm]
    local = [rhs_in, blob_in, cells_in, angles_in, self_in, near_in, weight_in, links_in, perm_in, interp_in, sibling_in, root_in]
    loads = [pltpu.make_async_copy(a, b, in_sem.at[i]) for i, (a, b) in enumerate(zip(hbm, local))]
    for load in loads:
        load.start()
    rhs_load, blob_load, cells_load, angles_load, self_load, near_load = loads[:6]

    def wrapped(index, shift, size):
        return lax.rem(index + shift + size, size)

    barrier = pltpu.get_barrier_semaphore()
    for shift in range(1, nx):
        pl.semaphore_signal(barrier, inc=1, device_id={"gx": wrapped(ix, shift, nx)}, device_id_type=MESH)
    for shift in range(1, ny):
        pl.semaphore_signal(barrier, inc=1, device_id={"gy": wrapped(iy, shift, ny)}, device_id_type=MESH)
    for shift in range(1, nz):
        pl.semaphore_signal(barrier, inc=1, device_id={"gz": iz ^ shift}, device_id_type=MESH)

    state_r[...] = jnp.zeros_like(state_r)
    rhs_load.wait()
    for c in range(3):
        state_r[c * PITCH : c * PITCH + BLOBS, :] = rhs_in[c]
    pl.semaphore_wait(barrier, nx + ny + nz - 3)

    def send(src, dst, send_sem, recv_sem, device):
        copy = pltpu.make_async_remote_copy(
            src_ref=src, dst_ref=dst, send_sem=send_sem, recv_sem=recv_sem, device_id=device, device_id_type=MESH
        )
        copy.start()
        pending.append(copy)
        return copy

    def send_box(phase, source, offset, device, copies):
        place = PLACE[offset]
        copies[offset] = send(
            source, halo.at[phase, place], rim_send.at[phase, place], rim_recv.at[phase, place], device
        )

    def start_halo(phase, state):
        rim[phase] = state[:, :128].T[:RIM]
        copies = {}
        own = rim.at[phase]
        send_box(phase, own, (0, -1), {"gy": wrapped(iy, 1, ny)}, copies)
        send_box(phase, own, (0, 1), {"gy": wrapped(iy, -1, ny)}, copies)
        send_box(phase, own, (-1, 0), {"gx": wrapped(ix, 1, nx)}, copies)
        send_box(phase, own, (1, 0), {"gx": wrapped(ix, -1, nx)}, copies)
        return copies

    def forward_halo(phase, copies, dy):
        copies[(0, dy)].wait_recv()
        box = halo.at[phase, PLACE[(0, dy)]]
        send_box(phase, box, (-1, dy), {"gx": wrapped(ix, 1, nx)}, copies)
        send_box(phase, box, (1, dy), {"gx": wrapped(ix, -1, nx)}, copies)

    def start_x(turn, value):
        stage_x[turn, 0] = value
        return [
            send(stage_x.at[turn, 0], stage_x.at[turn, d], x_send.at[turn, d], x_recv.at[turn, d], {"gx": wrapped(ix, d, nx)})
            for d in range(1, nx)
        ]

    def start_y(turn, value):
        stage_y[turn, 0] = value
        return [
            send(stage_y.at[turn, 0], stage_y.at[turn, d], y_send.at[turn, d], y_recv.at[turn, d], {"gy": wrapped(iy, d, ny)})
            for d in range(1, ny)
        ]

    def start_z(turn, value):
        stage_z[turn, 0] = value
        return [
            send(stage_z.at[turn, 0], stage_z.at[turn, d], z_send.at[turn, d], z_recv.at[turn, d], {"gz": iz ^ d})
            for d in range(1, nz)
        ]

    def summed(copies, stage, turn):
        for copy in copies:
            copy.wait_recv()
        return jnp.sum(stage[turn], axis=0)

    def charges(state):
        rows = [
            jnp.sum(blob_col[...] * state[c * PITCH : (c + 1) * PITCH, :], axis=0, keepdims=True) for c in range(3)
        ]
        moments = jnp.concatenate(rows + [jnp.zeros((5, BODIES), F32)], axis=0)
        return fold(mm(stacked(moments), occupancy[...], NT))

    def far_values(turn, copies):
        for copy in copies:
            copy.wait_recv()
        low_bit = lax.rem(iz, 2) == 1
        high_bit = iz // 2 == 1
        own, one, two, three = (stage_z[turn, d] for d in range(4))
        pick = lambda flag, a, b: jnp.where(flag, a, b)
        joined = jnp.concatenate(
            [
                jnp.concatenate([pick(low_bit, one, own), pick(low_bit, own, one)], axis=1),
                jnp.concatenate([pick(low_bit, three, two), pick(low_bit, two, three)], axis=1),
            ],
            axis=0,
        )
        up = [(up_op[0, level], up_op[1, level]) for level in range(2)]
        siblings = [(sibling_op[0, level], sibling_op[1, level]) for level in range(2)]
        first = mm_few(joined, up[0])
        mine, partner = first[:8], first[8:]
        second = jnp.concatenate([pick(high_bit, partner, mine), pick(high_bit, mine, partner)], axis=1)
        others = mm_few(second, up[1])
        potential = mm_few(others, (root_op[0], root_op[1]))
        placed = mm_few(potential, up[1], NT)
        potential = pick(high_bit, placed[:, CELLS:], placed[:, :CELLS])
        potential = potential + pltpu.roll(mm_few(partner, siblings[1]), 5, axis=0)
        placed = mm_few(potential, up[0], NT)
        potential = pick(low_bit, placed[:, CELLS:], placed[:, :CELLS])
        potential = potential + pltpu.roll(mm_few(one, siblings[0]), 5, axis=0)
        return fold(mm(stacked(potential), occupancy[...]))

    def factor(target, source, inverse):
        index = 3 * source + target if inverse else 3 * target + source
        return rotation[index : index + 1, :]

    def rotated(parts, inverse):
        return [
            factor(target, 0, inverse) * parts[0] + factor(target, 1, inverse) * parts[1] + factor(target, 2, inverse) * parts[2]
            for target in range(3)
        ]

    def write_self(state, result):
        parts = [state[c * PITCH : (c + 1) * PITCH, :] for c in range(3)]
        turned = jnp.concatenate(rotated(parts, False) + [jnp.zeros((ROWS - 3 * PITCH, BODIES), F32)], axis=0)
        mixture = mm3((self_op[0], self_op[1]), split(turned))
        back = rotated([mixture[c * PITCH : (c + 1) * PITCH] for c in range(3)], True)
        for c in range(3):
            result[c * PITCH : (c + 1) * PITCH, :] = back[c]
        result[3 * PITCH :, :] = jnp.zeros((ROWS - 3 * PITCH, BODIES), F32)

    def write_own_gather(state):
        own_gather[...] = mm3((link_op[0, :, :BODIES], link_op[1, :, :BODIES]), split(state[...]), NT)

    def finish(phase, result, values):
        boxes = split(halo[phase].reshape(NEIGH * RIM, ROWS))
        gathered = own_gather[...] + mm3((link_op[0, :, BODIES:], link_op[1, :, BODIES:]), boxes)
        result[...] += mm3((near_op[0], near_op[1]), split(gathered), NT)
        for c in range(3):
            result[c * PITCH : (c + 1) * PITCH, :] += blob_col[...] * values[c : c + 1, :]

    def write_operator(source, target):
        padded_mat[...] = jnp.zeros_like(padded_mat)
        for c in range(3):
            padded_mat[c * PITCH : c * PITCH + BLOBS, : 3 * BLOBS] = source[c * BLOBS : (c + 1) * BLOBS, :]
        matrix = padded_mat[...]
        lane = iota((ROWS, ROWS), 1)
        gap = PITCH - BLOBS
        spread = jnp.where(
            lane < PITCH, matrix, jnp.where(lane < 2 * PITCH, pltpu.roll(matrix, gap, axis=1), pltpu.roll(matrix, 2 * gap, axis=1))
        )
        target[0], target[1] = split(spread)

    def write_square(source, put):
        square[...] = jnp.zeros_like(square)
        square[:SKEL, :SKEL] = source
        put(square[...])

    halo_copies = start_halo(0, state_r)

    blob_load.wait()
    cells_load.wait()
    blob_row[...] = jnp.zeros_like(blob_row)
    blob_row[0:1, :BLOBS] = blob_in[...]
    diagonal = iota((PITCH, BODIES), 0) == iota((PITCH, BODIES), 1)
    column = jnp.sum(jnp.where(diagonal, blob_row[0:1, :], 0.0), axis=1, keepdims=True)
    blob_col[...] = jnp.broadcast_to(column, (PITCH, BODIES))
    occupancy[...] = jnp.where(iota((CELLS, BODIES), 0) == cells_in[...], 1.0, 0.0).astype(BF16)
    own_charges = charges(state_r)
    copies = start_x(0, own_charges)

    angles_load.wait()
    for target, row in enumerate(frame(angles_in[...])):
        for source, value in enumerate(row):
            rotation[3 * target + source : 3 * target + source + 1, :] = value
    self_load.wait()
    write_operator(self_in, self_op)

    copies = start_y(0, summed(copies, stage_x, 0))
    forward_halo(0, halo_copies, 1)

    for load in loads[8:]:
        load.wait()
    lane_few = iota((8, 512), 1)
    perm_row[...] = jnp.full_like(perm_row, -1.0)
    for level in range(2):
        perm = perm_in[level : level + 1, :].astype(F32)
        perm_row[level : level + 1, : 2 * SKEL] = jnp.where(perm >= SKEL, perm + (CELLS - SKEL), perm)
    perm_all = perm_row[...]
    kept_rows = jnp.where(lane_few < SKEL, perm_all, -1.0)[:, :CELLS]
    rest_rows = jnp.where(lane_few < SKEL, pltpu.roll(perm_all, 512 - SKEL, axis=1), -1.0)[:, :CELLS]
    for level in range(2):
        place = iota((2 * CELLS, CELLS), 0).astype(F32)
        kept = jnp.where(place == kept_rows[level : level + 1], 1.0, 0.0)
        rest = jnp.where(place == rest_rows[level : level + 1], 1.0, 0.0).astype(BF16)
        square[...] = jnp.zeros_like(square)
        square[:SKEL, :SKEL] = interp_in[level]
        high, low = split(square[...])
        up_op[0, level], up_op[1, level] = split(kept + (mm(rest, high) + mm(rest, low)))
        square[:SKEL, :SKEL] = sibling_in[level]
        sibling_op[0, level], sibling_op[1, level] = split(square[...])
    square[:SKEL, :SKEL] = root_in[...]
    root_op[0], root_op[1] = split(square[...])

    def start_far_z(turn, column_sum, own):
        return start_z(turn, (column_sum - own) + pltpu.roll(own, 3, axis=0))

    copies = start_far_z(0, summed(copies, stage_y, 0), own_charges)
    forward_halo(0, halo_copies, -1)

    near_load.wait()
    write_operator(near_in, near_op)
    loads[6].wait()
    loads[7].wait()
    links = links_in[...]
    box, body = links // BODIES, lax.rem(links, BODIES)
    place = jnp.where(box < 4, box, box - 1)
    lane_of = jnp.where(box == 4, body, BODIES + place * RIM + body)
    link_rows[...] = jnp.zeros_like(link_rows)
    link_rows[0:NEIGH, :] = lane_of.astype(F32)
    link_rows[NEIGH : 2 * NEIGH, :] = weight_in[...]
    link_cols[...] = link_rows[...].T
    block = 32

    @pl.loop(0, BODIES // block)
    def _(i):
        rows = pl.ds(pl.multiple_of(i * block, block), block)
        entries = link_cols[rows, :]
        width = BODIES + NEIGH * RIM
        lane = iota((block, width), 1).astype(F32)
        weights = jnp.zeros((block, width), F32)
        for k in range(NEIGH):
            weights = weights + jnp.where(lane == entries[:, k : k + 1], entries[:, NEIGH + k : NEIGH + k + 1], 0.0)
        link_op[0, rows, :], link_op[1, rows, :] = split(weights)

    write_self(state_r, state_u)
    write_own_gather(state_r)
    values = far_values(0, copies)
    for copy in halo_copies.values():
        if copy is not halo_copies[(0, 1)] and copy is not halo_copies[(0, -1)]:
            copy.wait_recv()
    finish(0, state_u, values)

    halo_copies = start_halo(1, state_u)
    own_charges = charges(state_u)
    copies = start_x(1, own_charges)
    for c in range(3):
        u_out[c] = state_u[c * PITCH : c * PITCH + BLOBS, :]
    store = pltpu.make_async_copy(u_out, u_hbm, out_sem)
    store.start()
    write_self(state_u, state_t)
    copies = start_y(1, summed(copies, stage_x, 1))
    write_own_gather(state_u)
    forward_halo(1, halo_copies, 1)

    tiny = 1e-30
    rr = total(state_r[...] * state_r[...])
    ru = total(state_r[...] * state_u[...])
    over_rr = jnp.where(rr > 0.0, 1.0 / jnp.where(rr > 0.0, rr, 1.0), 0.0)
    state_u[...] = state_u[...] - (ru * over_rr) * state_r[...]
    uu = total(state_u[...] * state_u[...])
    over_uu = jnp.where(uu > 0.0, 1.0 / jnp.where(uu > 0.0, uu, 1.0), 0.0)

    copies = start_far_z(1, summed(copies, stage_y, 1), own_charges)
    forward_halo(1, halo_copies, -1)
    values = far_values(1, copies)
    for copy in halo_copies.values():
        if copy is not halo_copies[(0, 1)] and copy is not halo_copies[(0, -1)]:
            copy.wait_recv()
    finish(1, state_t, values)

    largest = jnp.maximum(jnp.max(jnp.abs(state_t[...]), axis=(0, 1), keepdims=True), tiny)
    scaled = state_t[...] * (1.0 / largest)
    state_t[...] = scaled
    rt = total(state_r[...] * scaled)
    ut = total(state_u[...] * scaled)
    state_t[...] = state_t[...] - (rt * over_rr) * state_r[...] - (ut * over_uu) * state_u[...]
    tt = total(state_t[...] * state_t[...])
    root_rr, root_uu = jnp.sqrt(rr), jnp.sqrt(uu)
    triangle = [
        root_rr,
        ru * over_rr * root_rr,
        root_uu,
        largest * (rt * over_rr * root_rr),
        largest * (ut * over_uu * root_uu),
        largest * jnp.sqrt(tt),
    ]
    row_of = iota((8, 256), 0)
    lane_is_mine = iota((8, 256), 1) == ix + nx * (iy + ny * iz)
    tile = jnp.zeros((8, 256), F32)
    for i, value in enumerate(triangle):
        tile = jnp.where((row_of == i) & lane_is_mine, value, tile)
    copies = start_x(2, tile)
    copies = start_y(2, summed(copies, stage_x, 2))
    copies = start_z(2, summed(copies, stage_y, 2))
    everyone = summed(copies, stage_z, 2)

    r1, u1, u2, t1, t2, t3 = (everyone[i : i + 1] for i in range(6))
    dot = lambda *pairs: total(sum(a * b for a, b in pairs))
    beta = jnp.sqrt(dot((r1, r1)) + epsilon)
    v1 = r1 / beta
    image1, image2 = v1 + u1 / beta, u2 / beta
    diag_first = dot((image1, v1))
    w1, w2 = image1 - diag_first * v1, image2
    below_first = jnp.sqrt(dot((w1, w1), (w2, w2)) + epsilon)
    second1, second2 = w1 / below_first, w2 / below_first
    rest = (1.0 - diag_first) / beta
    z1 = second1 + (t1 / beta + rest * u1) / below_first
    z2 = second2 + (t2 / beta + rest * u2) / below_first
    z3 = (t3 / beta) / below_first
    above_second = dot((z1, v1))
    diag_second = dot((z1, second1), (z2, second2))
    left1 = z1 - above_second * v1 - diag_second * second1
    left2 = z2 - diag_second * second2
    below_second = jnp.sqrt(dot((left1, left1), (left2, left2), (z3, z3)) + epsilon)
    coef_one, coef_two, residual = least_squares(beta, diag_first, below_first, above_second, diag_second, below_second)
    on_r = coef_one / beta + coef_two * rest / below_first
    on_u = coef_two / (below_first * beta)
    row_few = iota((8, 128), 0)
    coef_ref[...] = jnp.where(row_few == 0, on_r, jnp.where(row_few == 1, on_u, residual))

    store.wait()
    for copy in pending:
        copy.wait_send()


def body(rhs, angles, self_mob, near_mat, near_weight, neighbours, cells, blob_weight, skel_perm, interp, sibling_ops, root_op):
    sizes = tuple(lax.axis_size(axis) for axis in ("gx", "gy", "gz"))
    nx, ny, nz = sizes
    initial = rhs.reshape(3, BLOBS, BODIES)
    operands = [
        initial,
        angles.reshape(3, BODIES),
        self_mob,
        near_mat,
        near_weight.reshape(NEIGH, BODIES),
        neighbours.reshape(NEIGH, BODIES),
        cells.reshape(1, BODIES),
        blob_weight.reshape(1, BLOBS),
        skel_perm,
        interp,
        sibling_ops,
        root_op,
    ]
    vmem = pltpu.VMEM
    dma = pltpu.SemaphoreType.DMA
    u, coefs = pl.pallas_call(
        lambda *refs: kernel(sizes, *refs),
        out_shape=(jax.ShapeDtypeStruct((3, BLOBS, BODIES), F32), jax.ShapeDtypeStruct((8, 128), F32)),
        in_specs=[pl.BlockSpec(memory_space=pl.ANY)] * len(operands),
        out_specs=(pl.BlockSpec(memory_space=pl.ANY), pl.BlockSpec(memory_space=pltpu.VMEM)),
        scratch_shapes=[vmem(x.shape, x.dtype) for x in operands]
        + [
            vmem((ROWS, BODIES), F32),
            vmem((ROWS, BODIES), F32),
            vmem((ROWS, BODIES), F32),
            vmem((ROWS, ROWS), F32),
            vmem((2, ROWS, ROWS), BF16),
            vmem((2, ROWS, ROWS), BF16),
            vmem((2, BODIES, BODIES + NEIGH * RIM), BF16),
            vmem((BODIES, 128), F32),
            vmem((128, BODIES), F32),
            vmem((CELLS, BODIES), BF16),
            vmem((8, BODIES), F32),
            vmem((PITCH, BODIES), F32),
            vmem((16, BODIES), F32),
            vmem((8, 512), F32),
            vmem((CELLS, CELLS), F32),
            vmem((2, 2, 2 * CELLS, CELLS), BF16),
            vmem((2, 2, CELLS, CELLS), BF16),
            vmem((2, CELLS, CELLS), BF16),
            vmem((BODIES, ROWS), F32),
            vmem((3, BLOBS, BODIES), F32),
            vmem((2, RIM, ROWS), F32),
            vmem((2, NEIGH, RIM, ROWS), F32),
            vmem((3, nx, 8, 256), F32),
            vmem((3, ny, 8, 256), F32),
            vmem((3, nz, 8, 256), F32),
            dma((len(operands),)),
            dma(()),
            dma((2, NEIGH)),
            dma((2, NEIGH)),
            dma((3, nx)),
            dma((3, nx)),
            dma((3, ny)),
            dma((3, ny)),
            dma((3, nz)),
            dma((3, nz)),
        ],
        compiler_params=pltpu.CompilerParams(collective_id=0, has_side_effects=True, vmem_limit_bytes=48 * 2**20),
    )(*operands)
    result = coefs[0, 0] * initial + coefs[1, 0] * u
    return (result[None, None], coefs[2, 0])


def solution(mesh):
    in_specs = (
        P("gx", "gy", None, None, "gz"),
        P("gx", "gy", None, "gz"),
        P(),
        P(),
        P("gx", "gy", None, "gz"),
        P("gx", "gy", None, "gz"),
        P("gx", "gy", "gz"),
        P(),
        P(),
        P(),
        P(),
        P(),
    )
    out_specs = (P("gx", "gy", None, None, "gz"), P())
    return jax.shard_map(body, mesh=mesh, in_specs=in_specs, out_specs=out_specs, check_vma=False)
```

```python
import jax
import jax.numpy as jnp
from jax import lax
from jax.experimental import pallas as pl
from jax.experimental.pallas import tpu as pltpu
from jax.sharding import PartitionSpec as P

F32 = jnp.float32
BF16 = jnp.bfloat16
MESH = pl.DeviceIdType.MESH
epsilon = 1e-06

BLOBS = 162
PITCH = 168
ROWS = 512
BODIES = 256
SKEL = 192
CELLS = 256
RIM = 64
NEIGH = 8
NN = (((1,), (0,)), ((), ()))
NT = (((1,), (1,)), ((), ()))
PARTS = 2


def split(x):
    high = x.astype(BF16)
    return high, (x - high.astype(F32)).astype(BF16)


def mm(a, b, dims=NN):
    return lax.dot_general(a, b, dims, preferred_element_type=F32)


def mm3(a, b, dims=NN):
    return mm(a[0], b[0], dims) + (mm(a[0], b[1], dims) + mm(a[1], b[0], dims))


def stacked(x):
    high = x.astype(BF16).astype(F32)
    return jnp.concatenate([high, x - high], axis=0).astype(BF16)


def fold(x):
    half = x.shape[0] // 2
    return x[:half] + x[half:]


def mm_few(x, weights, dims=NN):
    both = stacked(x)
    return fold(mm(both, weights[0], dims) + mm(both, weights[1], dims))


def total(x):
    return jnp.sum(x, axis=(0, 1), keepdims=True)


def iota(shape, dim):
    return lax.broadcasted_iota(jnp.int32, shape, dim)


def frame(angles):
    cos_all, sin_all = jnp.cos(angles), jnp.sin(angles)
    cy, cp, cr = cos_all[0:1], cos_all[1:2], cos_all[2:3]
    sy, sp, sr = sin_all[0:1], sin_all[1:2], sin_all[2:3]
    return (
        (cy * cp, cy * sp * sr - sy * cr, cy * sp * cr + sy * sr),
        (sy * cp, sy * sp * sr + cy * cr, sy * sp * cr - cy * sr),
        (-sp, cp * sr, cp * cr),
    )


def least_squares(beta, diag_first, below_first, above_second, diag_second, below_second):
    first_norm = jnp.sqrt(diag_first * diag_first + below_first * below_first)
    first_cos = diag_first / first_norm
    first_sin = below_first / first_norm
    top_right = first_cos * above_second + first_sin * diag_second
    lower_right = first_cos * diag_second - first_sin * above_second
    second_norm = jnp.sqrt(lower_right * lower_right + below_second * below_second)
    second_cos = lower_right / second_norm
    second_sin = below_second / second_norm
    carried = -first_sin * beta
    coef_two = second_cos * carried / second_norm
    coef_one = (first_cos * beta - top_right * coef_two) / first_norm
    return (coef_one, coef_two, jnp.abs(second_sin * carried))


CORE = [(0, 1, 0, 0, 0)]
PLANE = [(y, 0, x, 0, 0) for y in range(4) for x in range(4) if x or y]
DEPTH = [(0, 0, 0, low, high) for low in range(2) for high in range(4) if low or high]


def ring(step, size):
    return min(step % size, -step % size)


def hops(offset):
    y, _, x, low, high = offset
    return ring(y, 4) + ring(x, 4) + ring(2 * high + low, 8)


def kernel(
    rhs_hbm, angles_hbm, self_hbm, near_hbm, weight_hbm, links_hbm, cells_hbm, blob_hbm, perm_hbm, interp_hbm, sibling_hbm, root_hbm,
    u_hbm, on_r_ref, on_u_ref, residual_ref,
    rhs_in, angles_in, self_in, near_in, weight_in, links_in, cells_in, blob_in, perm_in, interp_in, sibling_in, root_in,
    state_r, state_u, state_t, padded_mat, self_op, near_op, link_op, link_cols, link_rows, occupancy, blob_row, blob_rows, blob_col,
    rotation, perm_row, square, up_op, sibling_op, root_op, own_gather, self_rim, u_out,
    rim, halo, stage_c, stage_p, stage_d,
    in_sem, out_sem, rim_send, rim_recv, c_send, c_recv, p_send, p_recv, d_send, d_recv,
):
    ix, iy, iz = lax.axis_index("gx"), lax.axis_index("gy"), lax.axis_index("gz")
    pending = []

    def body_rows(c):
        return slice(c * PITCH, c * PITCH + BLOBS)

    def pad_rows(c):
        return slice(c * PITCH + BLOBS, (c + 1) * PITCH if c < 2 else ROWS)

    for c in range(3):
        state_r[pad_rows(c), :] = jnp.zeros_like(state_r[pad_rows(c), :])
    pairs = {
        "rhs": (rhs_hbm.at[:, :, 0, :], rhs_in),
        "blob": (blob_hbm, blob_in),
        "cells": (cells_hbm, cells_in),
        "angles": (angles_hbm.at[:, 0, :], angles_in),
        "self": (self_hbm, self_in),
        "weight": (weight_hbm, weight_in),
        "links": (links_hbm, links_in),
        "perm": (perm_hbm, perm_in),
        "interp": (interp_hbm, interp_in),
        "sibling": (sibling_hbm, sibling_in),
        "root": (root_hbm, root_in),
        "near": (near_hbm, near_in),
    }
    loads = {name: pltpu.make_async_copy(a, b, in_sem.at[i]) for i, (name, (a, b)) in enumerate(pairs.items())}
    for load in loads.values():
        load.start()

    def wrapped(index, shift, size):
        return lax.rem(index + shift + size, size)

    odd = lax.rem(iy, 2)
    plus, minus = {"gx": wrapped(ix, 1, 8)}, {"gx": wrapped(ix, -1, 8)}
    across = {"gy": wrapped(iy, 2 * odd - 1, 8)}
    beside = {"gy": iy + 1 - 2 * odd}
    far_gx = {"gx": wrapped(ix, 2 * lax.rem(ix, 2) - 1, 8)}

    def peer(offset):
        y, core, x, low, high = offset
        device = {}
        if y or core:
            device["gx"] = 2 * lax.rem(ix // 2 + y, 4) + lax.rem(ix + core, 2)
        if x or low:
            device["gy"] = 2 * lax.rem(iy // 2 + x, 4) + lax.rem(iy + low, 2)
        if high:
            device["gz"] = iz ^ high
        return device

    barrier = pltpu.get_barrier_semaphore()
    greeted = [across, far_gx] + [peer(o) for o in sorted(DEPTH + PLANE + CORE, key=hops, reverse=True)]
    for device in greeted:
        pl.semaphore_signal(barrier, inc=1, device_id=device, device_id_type=MESH)

    def remote(src, dst, send_sem, recv_sem, device):
        return pltpu.make_async_remote_copy(
            src_ref=src, dst_ref=dst, send_sem=send_sem, recv_sem=recv_sem, device_id=device, device_id_type=MESH
        )

    def send(*what):
        copy = remote(*what)
        copy.start()
        pending.append(copy)
        return copy

    part = RIM // PARTS

    def box_copy(phase, source, place, i, device):
        rows = pl.ds(i * part, part)
        return (source.at[rows], halo.at[phase, place, rows], rim_send.at[phase, place, i], rim_recv.at[phase, place, i], device)

    def start_halo(phase):
        own = rim.at[phase]
        for i in range(PARTS):
            send(*box_copy(phase, own, 3 + odd, i, beside))
        for i in range(PARTS):
            send(*box_copy(phase, own, 4 - odd, i, across))
        for i in range(PARTS):
            send(*box_copy(phase, own, 1, i, plus))
            send(*box_copy(phase, own, 6, i, minus))

    def forward_halo(phase, place):
        box = halo.at[phase, place]
        for i in range(PARTS):
            remote(*box_copy(phase, rim.at[phase], place, i, plus)).wait_recv()
            send(*box_copy(phase, box, 2 * (place - 3), i, plus))
            send(*box_copy(phase, box, 2 * (place - 3) + 5, i, minus))

    def wait_boxes(phase):
        for place in (1, 6, 0, 5, 2, 7):
            for i in range(PARTS):
                remote(*box_copy(phase, rim.at[phase], place, i, plus)).wait_recv()

    def exchange(stage, send_sem, recv_sem, group, turn, value):
        stage[turn, 0] = value
        order = sorted(range(len(group)), key=lambda i: -hops(group[i]))
        copies = [
            send(stage.at[turn, 0], stage.at[turn, i + 1], send_sem.at[turn, i], recv_sem.at[turn, i], peer(group[i])) for i in order
        ]
        return copies[::-1]

    def start_core(turn, value):
        return exchange(stage_c, c_send, c_recv, CORE, turn, value)

    def start_plane(turn, value):
        return exchange(stage_p, p_send, p_recv, PLANE, turn, value)

    def start_depth(turn, value):
        return exchange(stage_d, d_send, d_recv, DEPTH, turn, value)

    def summed(copies, stage, turn):
        for copy in copies:
            copy.wait_recv()
        return jnp.sum(stage[turn], axis=0)

    def start_far(turn, copies, own):
        return start_depth(turn, summed(copies, stage_p, turn) + pltpu.roll(own, 3, axis=0))

    def charges(state):
        rows = [
            jnp.sum(blob_col[...] * state[c * PITCH : (c + 1) * PITCH, :], axis=0, keepdims=True) for c in range(3)
        ]
        moments = jnp.concatenate(rows + [jnp.zeros((5, BODIES), F32)], axis=0)
        return fold(mm(stacked(moments), occupancy[...], NT))

    def far_values(turn, copies):
        for copy in copies:
            copy.wait_recv()
        low_bit = lax.rem(iz, 2) == 1
        high_bit = iz // 2 == 1
        top = iota((8, CELLS), 0) < 3
        layers = []
        for high in range(4):
            here = stage_d[turn, DEPTH.index((0, 0, 0, 0, high)) + 1 if high else 0]
            there = stage_d[turn, DEPTH.index((0, 0, 0, 1, high)) + 1]
            layers.append(jnp.where(top, here + there - pltpu.roll(here, 5, axis=0), here))
        own, one, two, three = layers
        pick = lambda flag, a, b: jnp.where(flag, a, b)
        joined = jnp.concatenate(
            [
                jnp.concatenate([pick(low_bit, one, own), pick(low_bit, own, one)], axis=1),
                jnp.concatenate([pick(low_bit, three, two), pick(low_bit, two, three)], axis=1),
            ],
            axis=0,
        )
        up = [(up_op[0, level], up_op[1, level]) for level in range(2)]
        siblings = [(sibling_op[0, level], sibling_op[1, level]) for level in range(2)]
        first = mm_few(joined, up[0])
        mine, partner = first[:8], first[8:]
        second = jnp.concatenate([pick(high_bit, partner, mine), pick(high_bit, mine, partner)], axis=1)
        others = mm_few(second, up[1])
        potential = mm_few(others, (root_op[0], root_op[1]))
        placed = mm_few(potential, up[1], NT)
        potential = pick(high_bit, placed[:, CELLS:], placed[:, :CELLS])
        potential = potential + pltpu.roll(mm_few(partner, siblings[1]), 5, axis=0)
        placed = mm_few(potential, up[0], NT)
        potential = pick(low_bit, placed[:, CELLS:], placed[:, :CELLS])
        potential = potential + pltpu.roll(mm_few(one, siblings[0]), 5, axis=0)
        return fold(mm(stacked(potential), occupancy[...]))

    def factor(target, source, inverse):
        index = 3 * source + target if inverse else 3 * target + source
        return rotation[index : index + 1, :]

    def rotated(parts, inverse):
        return [
            factor(target, 0, inverse) * parts[0] + factor(target, 1, inverse) * parts[1] + factor(target, 2, inverse) * parts[2]
            for target in range(3)
        ]

    def write_self(state, result):
        parts = [state[c * PITCH : (c + 1) * PITCH, :] for c in range(3)]
        turned = jnp.concatenate(rotated(parts, False) + [jnp.zeros((ROWS - 3 * PITCH, BODIES), F32)], axis=0)
        mixture = mm3((self_op[0], self_op[1]), split(turned))
        back = rotated([mixture[c * PITCH : (c + 1) * PITCH] for c in range(3)], True)
        for c in range(3):
            result[c * PITCH : (c + 1) * PITCH, :] = back[c]
        result[3 * PITCH :, :] = jnp.zeros((ROWS - 3 * PITCH, BODIES), F32)

    def write_own_gather(state):
        own_gather[...] = mm3((link_op[0, :, :BODIES], link_op[1, :, :BODIES]), split(state[...]), NT)

    def boxes_of(phase):
        return split(halo[phase].reshape(NEIGH * RIM, ROWS))

    def gathered(bodies, boxes):
        return own_gather[:bodies, :] + mm3((link_op[0, :bodies, BODIES:], link_op[1, :bodies, BODIES:]), boxes)

    def near_pair():
        return (near_op[0], near_op[1])

    def finish(result, boxes, values):
        result[...] += mm3(near_pair(), split(gathered(BODIES, boxes)), NT)
        for c in range(3):
            result[c * PITCH : (c + 1) * PITCH, :] += blob_col[...] * values[c : c + 1, :]

    def write_operator(source, target):
        padded_mat[...] = jnp.zeros_like(padded_mat)
        for c in range(3):
            padded_mat[c * PITCH : c * PITCH + BLOBS, : 3 * BLOBS] = source[c * BLOBS : (c + 1) * BLOBS, :]
        matrix = padded_mat[...]
        lane = iota((ROWS, ROWS), 1)
        gap = PITCH - BLOBS
        spread = jnp.where(
            lane < PITCH, matrix, jnp.where(lane < 2 * PITCH, pltpu.roll(matrix, gap, axis=1), pltpu.roll(matrix, 2 * gap, axis=1))
        )
        target[0], target[1] = split(spread)

    loads["rhs"].wait()
    for c in range(3):
        state_r[body_rows(c), :] = rhs_in[c]
    rim[0] = state_r[:, :128].T[:RIM]
    pl.semaphore_wait(barrier, len(greeted))
    start_halo(0)

    loads["blob"].wait()
    loads["cells"].wait()
    blob_row[...] = jnp.zeros_like(blob_row)
    blob_row[0:1, :BLOBS] = blob_in[...]
    diagonal = iota((PITCH, BODIES), 0) == iota((PITCH, BODIES), 1)
    column = jnp.sum(jnp.where(diagonal, blob_row[0:1, :BODIES], 0.0), axis=1, keepdims=True)
    blob_col[...] = jnp.broadcast_to(column, (PITCH, BODIES))
    occupancy[...] = jnp.where(iota((CELLS, BODIES), 0) == cells_in[...], 1.0, 0.0).astype(BF16)
    own_charges = charges(state_r)
    copies = start_core(0, own_charges)

    loads["angles"].wait()
    for target, row in enumerate(frame(angles_in[...])):
        for source, value in enumerate(row):
            rotation[3 * target + source : 3 * target + source + 1, :] = value
    copies = start_plane(0, summed(copies, stage_c, 0))
    loads["self"].wait()
    write_operator(self_in, self_op)

    for name in ("perm", "interp", "sibling", "root"):
        loads[name].wait()
    lane_few = iota((8, 512), 1)
    blob_first = blob_row[...]
    for c in range(3):
        blob_rows[c : c + 1, :] = pltpu.roll(blob_first, c * PITCH, axis=1)[0:1] if c else blob_first[0:1]
    perm_row[...] = jnp.full_like(perm_row, -1.0)
    for level in range(2):
        perm = perm_in[level : level + 1, :].astype(F32)
        perm_row[level : level + 1, : 2 * SKEL] = jnp.where(perm >= SKEL, perm + (CELLS - SKEL), perm)
    perm_all = perm_row[...]
    kept_rows = jnp.where(lane_few < SKEL, perm_all, -1.0)[:, :CELLS]
    rest_rows = jnp.where(lane_few < SKEL, pltpu.roll(perm_all, 512 - SKEL, axis=1), -1.0)[:, :CELLS]
    square[...] = jnp.zeros_like(square)
    for level in range(2):
        place = iota((2 * CELLS, CELLS), 0).astype(F32)
        kept = jnp.where(place == kept_rows[level : level + 1], 1.0, 0.0)
        rest = jnp.where(place == rest_rows[level : level + 1], 1.0, 0.0).astype(BF16)
        square[:SKEL, :SKEL] = interp_in[level]
        high, low = split(square[...])
        up_op[0, level], up_op[1, level] = split(kept + (mm(rest, high) + mm(rest, low)))
        square[:SKEL, :SKEL] = sibling_in[level]
        sibling_op[0, level], sibling_op[1, level] = split(square[...])
    square[:SKEL, :SKEL] = root_in[...]
    root_op[0], root_op[1] = split(square[...])

    forward_halo(0, 4 - odd)
    copies = start_far(0, copies, own_charges)
    write_self(state_r, state_u)
    self_rim[...] = state_u[:, :128].T[:RIM]
    forward_halo(0, 3 + odd)

    loads["weight"].wait()
    loads["links"].wait()
    links = links_in[...]
    box, body = links // BODIES, lax.rem(links, BODIES)
    place = jnp.where(box < 4, box, box - 1)
    lane_of = jnp.where(box == 4, body, BODIES + place * RIM + body)
    link_rows[...] = jnp.zeros_like(link_rows)
    link_rows[0:NEIGH, :] = lane_of.astype(F32)
    link_rows[NEIGH : 2 * NEIGH, :] = weight_in[...]
    link_cols[...] = link_rows[...].T
    block = 32

    @pl.loop(0, BODIES // block)
    def _(i):
        rows = pl.ds(pl.multiple_of(i * block, block), block)
        entries = link_cols[rows, :]
        width = BODIES + NEIGH * RIM
        lane = iota((block, width), 1).astype(F32)
        weights = jnp.zeros((block, width), F32)
        for k in range(NEIGH):
            weights = weights + jnp.where(lane == entries[:, k : k + 1], entries[:, NEIGH + k : NEIGH + k + 1], 0.0)
        link_op[0, rows, :], link_op[1, rows, :] = split(weights)

    loads["near"].wait()
    write_operator(near_in, near_op)
    write_own_gather(state_r)
    values = far_values(0, copies)
    wait_boxes(0)

    boxes = boxes_of(0)
    columns = jnp.concatenate([values, jnp.zeros((120, BODIES), F32)], axis=0)[:, :128].T[:RIM]
    far_rim = sum(columns[:, c : c + 1] * blob_rows[c : c + 1, :] for c in range(3))
    rim[1] = self_rim[...] + mm3(split(gathered(RIM, boxes)), near_pair(), NT) + far_rim
    start_halo(1)
    finish(state_u, boxes, values)
    own_charges = charges(state_u)
    copies = start_core(1, own_charges)
    for c in range(3):
        u_out[c] = state_u[body_rows(c), :]
    store = pltpu.make_async_copy(u_out, u_hbm.at[:, :, 0, :], out_sem)
    store.start()
    write_self(state_u, state_t)
    copies = start_plane(1, summed(copies, stage_c, 1))
    forward_halo(1, 4 - odd)
    write_own_gather(state_u)

    tiny = 1e-30
    rr = total(state_r[...] * state_r[...])
    ru = total(state_r[...] * state_u[...])
    over_rr = jnp.where(rr > 0.0, 1.0 / jnp.where(rr > 0.0, rr, 1.0), 0.0)
    forward_halo(1, 3 + odd)
    state_u[...] = state_u[...] - (ru * over_rr) * state_r[...]
    uu = total(state_u[...] * state_u[...])
    over_uu = jnp.where(uu > 0.0, 1.0 / jnp.where(uu > 0.0, uu, 1.0), 0.0)

    copies = start_far(1, copies, own_charges)
    values = far_values(1, copies)
    wait_boxes(1)
    finish(state_t, boxes_of(1), values)

    largest = jnp.maximum(jnp.max(jnp.abs(state_t[...]), axis=(0, 1), keepdims=True), tiny)
    scaled = state_t[...] * (1.0 / largest)
    state_t[...] = scaled
    rt = total(state_r[...] * scaled)
    ut = total(state_u[...] * scaled)
    state_t[...] = state_t[...] - (rt * over_rr) * state_r[...] - (ut * over_uu) * state_u[...]
    tt = total(state_t[...] * state_t[...])
    root_rr, root_uu = jnp.sqrt(rr), jnp.sqrt(uu)
    triangle = [
        root_rr,
        ru * over_rr * root_rr,
        root_uu,
        largest * (rt * over_rr * root_rr),
        largest * (ut * over_uu * root_uu),
        largest * jnp.sqrt(tt),
    ]
    row_of = iota((8, 256), 0)
    lane_is_mine = iota((8, 256), 1) == ix + 8 * (iy + 8 * iz)
    tile = jnp.zeros((8, 256), F32)
    for i, value in enumerate(triangle):
        tile = jnp.where((row_of == i) & lane_is_mine, value, tile)
    copies = start_core(2, tile)
    copies = start_plane(2, summed(copies, stage_c, 2))
    copies = start_depth(2, summed(copies, stage_p, 2))
    everyone = summed(copies, stage_d, 2)

    r1, u1, u2, t1, t2, t3 = (everyone[i : i + 1] for i in range(6))
    dot = lambda *pairs: total(sum(a * b for a, b in pairs))
    beta = jnp.sqrt(dot((r1, r1)) + epsilon)
    v1 = r1 / beta
    image1, image2 = v1 + u1 / beta, u2 / beta
    diag_first = dot((image1, v1))
    w1, w2 = image1 - diag_first * v1, image2
    below_first = jnp.sqrt(dot((w1, w1), (w2, w2)) + epsilon)
    second1, second2 = w1 / below_first, w2 / below_first
    rest = (1.0 - diag_first) / beta
    z1 = second1 + (t1 / beta + rest * u1) / below_first
    z2 = second2 + (t2 / beta + rest * u2) / below_first
    z3 = (t3 / beta) / below_first
    above_second = dot((z1, v1))
    diag_second = dot((z1, second1), (z2, second2))
    left1 = z1 - above_second * v1 - diag_second * second1
    left2 = z2 - diag_second * second2
    below_second = jnp.sqrt(dot((left1, left1), (left2, left2), (z3, z3)) + epsilon)
    coef_one, coef_two, residual = least_squares(beta, diag_first, below_first, above_second, diag_second, below_second)
    on_r = coef_one / beta + coef_two * rest / below_first
    on_u = coef_two / (below_first * beta)
    on_r_ref[...] = jnp.broadcast_to(on_r, (1, BODIES))
    on_u_ref[...] = jnp.broadcast_to(on_u, (1, BODIES))
    residual_ref[...] = residual

    store.wait()
    for copy in pending:
        copy.wait_send()


def body(rhs, angles, self_mob, near_mat, near_weight, neighbours, cells, blob_weight, skel_perm, interp, sibling_ops, root_op):
    initial = rhs.reshape(3, BLOBS, 1, BODIES)
    operands = [
        initial,
        angles.reshape(3, 1, BODIES),
        self_mob,
        near_mat,
        near_weight.reshape(NEIGH, BODIES),
        neighbours.reshape(NEIGH, BODIES),
        cells.reshape(1, BODIES),
        blob_weight.reshape(1, BLOBS),
        skel_perm,
        interp,
        sibling_ops,
        root_op,
    ]
    vmem = pltpu.VMEM
    dma = pltpu.SemaphoreType.DMA
    u, on_r, on_u, residual = pl.pallas_call(
        kernel,
        out_shape=(
            jax.ShapeDtypeStruct(initial.shape, F32),
            jax.ShapeDtypeStruct((1, BODIES), F32),
            jax.ShapeDtypeStruct((1, BODIES), F32),
            jax.ShapeDtypeStruct((1, 1), F32),
        ),
        in_specs=[pl.BlockSpec(memory_space=pltpu.HBM)] * len(operands),
        out_specs=(
            pl.BlockSpec(memory_space=pltpu.HBM),
            pl.BlockSpec(memory_space=pltpu.VMEM),
            pl.BlockSpec(memory_space=pltpu.VMEM),
            pl.BlockSpec(memory_space=pltpu.VMEM),
        ),
        scratch_shapes=[vmem((3, BLOBS, BODIES), F32), vmem((3, BODIES), F32)]
        + [vmem(x.shape, x.dtype) for x in operands[2:]]
        + [
            vmem((ROWS, BODIES), F32),
            vmem((ROWS, BODIES), F32),
            vmem((ROWS, BODIES), F32),
            vmem((ROWS, ROWS), F32),
            vmem((2, ROWS, ROWS), BF16),
            vmem((2, ROWS, ROWS), BF16),
            vmem((2, BODIES, BODIES + NEIGH * RIM), BF16),
            vmem((BODIES, 128), F32),
            vmem((128, BODIES), F32),
            vmem((CELLS, BODIES), BF16),
            vmem((8, ROWS), F32),
            vmem((8, ROWS), F32),
            vmem((PITCH, BODIES), F32),
            vmem((16, BODIES), F32),
            vmem((8, 512), F32),
            vmem((CELLS, CELLS), F32),
            vmem((2, 2, 2 * CELLS, CELLS), BF16),
            vmem((2, 2, CELLS, CELLS), BF16),
            vmem((2, CELLS, CELLS), BF16),
            vmem((BODIES, ROWS), F32),
            vmem((RIM, ROWS), F32),
            vmem((3, BLOBS, BODIES), F32),
            vmem((2, RIM, ROWS), F32),
            vmem((2, NEIGH, RIM, ROWS), F32),
            vmem((3, len(CORE) + 1, 8, 256), F32),
            vmem((3, len(PLANE) + 1, 8, 256), F32),
            vmem((3, len(DEPTH) + 1, 8, 256), F32),
            dma((len(operands),)),
            dma(()),
            dma((2, NEIGH, PARTS)),
            dma((2, NEIGH, PARTS)),
            dma((3, len(CORE))),
            dma((3, len(CORE))),
            dma((3, len(PLANE))),
            dma((3, len(PLANE))),
            dma((3, len(DEPTH))),
            dma((3, len(DEPTH))),
        ],
        compiler_params=pltpu.CompilerParams(collective_id=0, has_side_effects=True, vmem_limit_bytes=64 * 2**20),
    )(*operands)
    result = on_r * initial + on_u * u
    return (result.reshape(rhs.shape), residual.reshape(()))


def solution(mesh):
    in_specs = (
        P("gx", "gy", None, None, "gz"),
        P("gx", "gy", None, "gz"),
        P(),
        P(),
        P("gx", "gy", None, "gz"),
        P("gx", "gy", None, "gz"),
        P("gx", "gy", "gz"),
        P(),
        P(),
        P(),
        P(),
        P(),
    )
    out_specs = (P("gx", "gy", None, None, "gz"), P())
    return jax.shard_map(body, mesh=mesh, in_specs=in_specs, out_specs=out_specs, check_vma=False)
```

```python
import jax
import jax.numpy as jnp
from jax import lax
from jax.experimental import pallas as pl
from jax.experimental.pallas import tpu as pltpu
from jax.sharding import PartitionSpec as P

F32 = jnp.float32
BF16 = jnp.bfloat16
MESH = pl.DeviceIdType.MESH
epsilon = 1e-06

BLOBS = 162
PITCH = 168
ROWS = 512
BODIES = 256
SKEL = 192
CELLS = 256
RIM = 64
NEIGH = 8
NN = (((1,), (0,)), ((), ()))
NT = (((1,), (1,)), ((), ()))
PARTS = 2
PLACES = {1: 0, 3: 1, 5: 2, 7: 3, 0: 4, 2: 5, 6: 6, 8: 7}


def split(x):
    high = x.astype(BF16)
    return high, (x - high.astype(F32)).astype(BF16)


def mm(a, b, dims=NN):
    return lax.dot_general(a, b, dims, preferred_element_type=F32)


def mm3(a, b, dims=NN):
    return mm(a[0], b[0], dims) + (mm(a[0], b[1], dims) + mm(a[1], b[0], dims))


def stacked(x):
    high = x.astype(BF16).astype(F32)
    return jnp.concatenate([high, x - high], axis=0).astype(BF16)


def fold(x):
    half = x.shape[0] // 2
    return x[:half] + x[half:]


def mm_few(x, weights, dims=NN):
    both = stacked(x)
    return fold(mm(both, weights[0], dims) + mm(both, weights[1], dims))


def total(x):
    return jnp.sum(x, axis=(0, 1), keepdims=True)


def iota(shape, dim):
    return lax.broadcasted_iota(jnp.int32, shape, dim)


def frame(angles):
    cos_all, sin_all = jnp.cos(angles), jnp.sin(angles)
    cy, cp, cr = cos_all[0:1], cos_all[1:2], cos_all[2:3]
    sy, sp, sr = sin_all[0:1], sin_all[1:2], sin_all[2:3]
    return (
        (cy * cp, cy * sp * sr - sy * cr, cy * sp * cr + sy * sr),
        (sy * cp, sy * sp * sr + cy * cr, sy * sp * cr - cy * sr),
        (-sp, cp * sr, cp * cr),
    )


def least_squares(beta, diag_first, below_first, above_second, diag_second, below_second):
    first_norm = jnp.sqrt(diag_first * diag_first + below_first * below_first)
    first_cos = diag_first / first_norm
    first_sin = below_first / first_norm
    top_right = first_cos * above_second + first_sin * diag_second
    lower_right = first_cos * diag_second - first_sin * above_second
    second_norm = jnp.sqrt(lower_right * lower_right + below_second * below_second)
    second_cos = lower_right / second_norm
    second_sin = below_second / second_norm
    carried = -first_sin * beta
    coef_two = second_cos * carried / second_norm
    coef_one = (first_cos * beta - top_right * coef_two) / first_norm
    return (coef_one, coef_two, jnp.abs(second_sin * carried))


CORE = [(0, 1, 0, 0, 0)]
PLANE = [(y, 0, x, 0, 0) for y in range(4) for x in range(4) if x or y]
DEPTH = [(0, 0, 0, low, high) for low in range(2) for high in range(4) if low or high]


def ring(step, size):
    return min(step % size, -step % size)


def hops(offset):
    y, _, x, low, high = offset
    return ring(y, 4) + ring(x, 4) + ring(2 * high + low, 8)


def kernel(
    rhs_hbm, angles_hbm, self_hbm, near_hbm, weight_hbm, links_hbm, cells_hbm, blob_hbm, perm_hbm, interp_hbm, sibling_hbm, root_hbm,
    result_hbm, residual_ref,
    rhs_in, angles_in, self_in, near_in, weight_in, links_in, cells_in, blob_in, perm_in, interp_in, sibling_in, root_in,
    state_r, state_u, state_t, padded_mat, self_op, near_op, link_op, link_cols, link_rows, occupancy, blob_row, blob_rows, blob_col,
    rotation, perm_row, square, up_op, down_op, sibling_op, root_op, own_gather, self_rim, u_out,
    rim, halo, stage_c, stage_p, stage_d,
    in_sem, out_sem, rim_send, rim_recv, c_send, c_recv, p_send, p_recv, d_send, d_recv,
):
    ix, iy, iz = lax.axis_index("gx"), lax.axis_index("gy"), lax.axis_index("gz")
    pending = []

    def body_rows(c):
        return slice(c * PITCH, c * PITCH + BLOBS)

    def pad_rows(c):
        return slice(c * PITCH + BLOBS, (c + 1) * PITCH if c < 2 else ROWS)

    for c in range(3):
        state_r[pad_rows(c), :] = jnp.zeros_like(state_r[pad_rows(c), :])
    pairs = {
        "rhs": (rhs_hbm.at[:, :, 0, :], rhs_in),
        "blob": (blob_hbm, blob_in),
        "cells": (cells_hbm, cells_in),
        "angles": (angles_hbm.at[:, 0, :], angles_in),
        "self": (self_hbm, self_in),
        "weight": (weight_hbm, weight_in),
        "links": (links_hbm, links_in),
        "perm": (perm_hbm, perm_in),
        "interp": (interp_hbm, interp_in),
        "sibling": (sibling_hbm, sibling_in),
        "root": (root_hbm, root_in),
        "near": (near_hbm, near_in),
    }
    loads = {name: pltpu.make_async_copy(a, b, in_sem.at[i]) for i, (name, (a, b)) in enumerate(pairs.items())}
    for load in loads.values():
        load.start()

    def wrapped(index, shift, size):
        return lax.rem(index + shift + size, size)

    odd = lax.rem(iy, 2)
    plus, minus = {"gx": wrapped(ix, 1, 8)}, {"gx": wrapped(ix, -1, 8)}
    across = {"gy": wrapped(iy, 2 * odd - 1, 8)}
    beside = {"gy": iy + 1 - 2 * odd}
    far_gx = {"gx": wrapped(ix, 2 * lax.rem(ix, 2) - 1, 8)}

    known = {}

    def peer(offset):
        if offset not in known:
            known[offset] = device_at(offset)
        return known[offset]

    def device_at(offset):
        y, core, x, low, high = offset
        device = {}
        if y or core:
            device["gx"] = 2 * lax.rem(ix // 2 + y, 4) + lax.rem(ix + core, 2)
        if x or low:
            device["gy"] = 2 * lax.rem(iy // 2 + x, 4) + lax.rem(iy + low, 2)
        if high:
            device["gz"] = iz ^ high
        return device

    barrier = pltpu.get_barrier_semaphore()
    greeted = [across, far_gx] + [peer(o) for o in sorted(DEPTH + PLANE + CORE, key=hops, reverse=True)]
    for device in greeted:
        pl.semaphore_signal(barrier, inc=1, device_id=device, device_id_type=MESH)

    def remote(src, dst, send_sem, recv_sem, device):
        return pltpu.make_async_remote_copy(
            src_ref=src, dst_ref=dst, send_sem=send_sem, recv_sem=recv_sem, device_id=device, device_id_type=MESH
        )

    def send(*what):
        copy = remote(*what)
        copy.start()
        pending.append(copy)
        return copy

    def drain():
        for copy in pending:
            copy.wait_send()
        pending.clear()

    part = RIM // PARTS

    def box_copy(phase, source, place, i, device):
        rows = pl.ds(i * part, part)
        return (source.at[rows], halo.at[phase, place, rows], rim_send.at[phase, place, i], rim_recv.at[phase, place, i], device)

    def start_halo(phase):
        own = rim.at[phase]
        for i in range(PARTS):
            send(*box_copy(phase, own, 1 + odd, i, beside))
        for i in range(PARTS):
            send(*box_copy(phase, own, 2 - odd, i, across))
        for i in range(PARTS):
            send(*box_copy(phase, own, 0, i, plus))
            send(*box_copy(phase, own, 3, i, minus))

    def forward_halo(phase, place):
        box = halo.at[phase, place]
        for i in range(PARTS):
            remote(*box_copy(phase, rim.at[phase], place, i, plus)).wait_recv()
            send(*box_copy(phase, box, place + 3, i, plus))
            send(*box_copy(phase, box, place + 5, i, minus))

    def wait_boxes(phase, places):
        for place in places:
            for i in range(PARTS):
                remote(*box_copy(phase, rim.at[phase], place, i, plus)).wait_recv()

    def exchange(stage, send_sem, recv_sem, group, turn, value):
        stage[turn, 0] = value
        order = sorted(range(len(group)), key=lambda i: -hops(group[i]))
        copies = [
            send(stage.at[turn, 0], stage.at[turn, i + 1], send_sem.at[turn, i], recv_sem.at[turn, i], peer(group[i])) for i in order
        ]
        return copies[::-1]

    def start_core(turn, value):
        return exchange(stage_c, c_send, c_recv, CORE, turn, value)

    def start_plane(turn, value):
        return exchange(stage_p, p_send, p_recv, PLANE, turn, value)

    def start_depth(turn, value):
        return exchange(stage_d, d_send, d_recv, DEPTH, turn, value)

    def summed(copies, stage, turn):
        for copy in copies:
            copy.wait_recv()
        return jnp.sum(stage[turn], axis=0)

    def start_far(turn, copies, own):
        return start_depth(turn, summed(copies, stage_p, turn) + pltpu.roll(own, 3, axis=0))

    def moments_of(state):
        rows = [
            jnp.sum(blob_col[...] * state[c * PITCH : (c + 1) * PITCH, :], axis=0, keepdims=True) for c in range(3)
        ]
        return jnp.concatenate(rows + [jnp.zeros((5, BODIES), F32)], axis=0)

    def charges(moments):
        return fold(mm(stacked(moments), occupancy[...], NT))

    low_bit = lax.rem(iz, 2) == 1
    high_bit = iz // 2 == 1

    def pick(flag, a, b):
        return jnp.where(flag, a, b)

    def pair(ref):
        return (ref[0], ref[1])

    def far_values(turn, copies):
        for copy in copies:
            copy.wait_recv()
        top = iota((8, CELLS), 0) < 3
        layers = []
        for high in range(4):
            here = stage_d[turn, DEPTH.index((0, 0, 0, 0, high)) + 1 if high else 0]
            there = stage_d[turn, DEPTH.index((0, 0, 0, 1, high)) + 1]
            layers.append(jnp.where(top, here + there - pltpu.roll(here, 5, axis=0), here))
        own, one, two, three = layers
        joined = jnp.concatenate(
            [
                jnp.concatenate([pick(low_bit, one, own), pick(low_bit, own, one)], axis=1),
                jnp.concatenate([pick(low_bit, three, two), pick(low_bit, two, three)], axis=1),
            ],
            axis=0,
        )
        first = mm_few(joined, pair(up_op))
        mine, partner = first[:8], first[8:]
        second = jnp.concatenate([pick(high_bit, partner, mine), pick(high_bit, mine, partner)], axis=1)
        potential = mm_few(second, pair(root_op)) + pltpu.roll(mm_few(partner, pair(sibling_op.at[1])), 5, axis=0)
        potential = mm_few(potential, pair(down_op), NT) + pltpu.roll(mm_few(one, pair(sibling_op.at[0])), 5, axis=0)
        return jnp.where(top, fold(mm(stacked(potential), occupancy[...])), 0.0)

    def factor(target, source, inverse):
        index = 3 * source + target if inverse else 3 * target + source
        return rotation[index : index + 1, :]

    def rotated(parts, inverse):
        return [
            factor(target, 0, inverse) * parts[0] + factor(target, 1, inverse) * parts[1] + factor(target, 2, inverse) * parts[2]
            for target in range(3)
        ]

    def write_self(state, result):
        parts = [state[c * PITCH : (c + 1) * PITCH, :] for c in range(3)]
        turned = jnp.concatenate(rotated(parts, False) + [jnp.zeros((ROWS - 3 * PITCH, BODIES), F32)], axis=0)
        mixture = mm3((self_op[0], self_op[1]), split(turned))
        back = rotated([mixture[c * PITCH : (c + 1) * PITCH] for c in range(3)], True)
        for c in range(3):
            result[c * PITCH : (c + 1) * PITCH, :] = back[c]
        result[3 * PITCH :, :] = jnp.zeros((ROWS - 3 * PITCH, BODIES), F32)

    def write_own_gather(state):
        own_gather[...] = mm3((link_op[0, :, :BODIES], link_op[1, :, :BODIES]), split(state[...]), NT)

    def add_boxes(phase, first, last):
        lanes = slice(BODIES + first * RIM, BODIES + last * RIM)
        boxes = split(halo[phase, first:last].reshape((last - first) * RIM, ROWS))
        return own_gather[...] + mm3((link_op[0, :, lanes], link_op[1, :, lanes]), boxes)

    def add_far(result, values):
        for c in range(3):
            result[c * PITCH : (c + 1) * PITCH, :] += blob_col[...] * values[c : c + 1, :]

    def write_operator(source, target):
        padded_mat[...] = jnp.zeros_like(padded_mat)
        for c in range(3):
            padded_mat[c * PITCH : c * PITCH + BLOBS, : 3 * BLOBS] = source[c * BLOBS : (c + 1) * BLOBS, :]
        matrix = padded_mat[...]
        lane = iota((ROWS, ROWS), 1)
        gap = PITCH - BLOBS
        spread = jnp.where(
            lane < PITCH, matrix, jnp.where(lane < 2 * PITCH, pltpu.roll(matrix, gap, axis=1), pltpu.roll(matrix, 2 * gap, axis=1))
        )
        target[0], target[1] = split(spread)

    loads["rhs"].wait()
    for c in range(3):
        state_r[body_rows(c), :] = rhs_in[c]
    rim[0] = state_r[:, :128].T[:RIM]
    loads["weight"].wait()
    loads["links"].wait()
    links = links_in[...]
    box, body = links // BODIES, lax.rem(links, BODIES)
    place = jnp.zeros_like(box)
    for slot, index in PLACES.items():
        place = jnp.where(box == slot, index, place)
    lane_of = jnp.where(box == 4, body, BODIES + place * RIM + body)
    link_rows[...] = jnp.zeros_like(link_rows)
    link_rows[0:NEIGH, :] = lane_of.astype(F32)
    link_rows[NEIGH : 2 * NEIGH, :] = weight_in[...]
    link_cols[...] = link_rows[...].T
    block = 32

    @pl.loop(0, BODIES // block)
    def _(i):
        rows = pl.ds(pl.multiple_of(i * block, block), block)
        entries = link_cols[rows, :]
        width = BODIES + NEIGH * RIM
        lane = iota((block, width), 1).astype(F32)
        weights = jnp.zeros((block, width), F32)
        for k in range(NEIGH):
            weights = weights + jnp.where(lane == entries[:, k : k + 1], entries[:, NEIGH + k : NEIGH + k + 1], 0.0)
        link_op[0, rows, :], link_op[1, rows, :] = split(weights)

    pl.semaphore_wait(barrier, len(greeted))
    start_halo(0)

    loads["blob"].wait()
    loads["cells"].wait()
    blob_row[...] = jnp.zeros_like(blob_row)
    blob_row[0:1, :BLOBS] = blob_in[...]
    diagonal = iota((PITCH, BODIES), 0) == iota((PITCH, BODIES), 1)
    blob_square = total(blob_row[0:1, :] * blob_row[0:1, :])
    column = jnp.sum(jnp.where(diagonal, blob_row[0:1, :BODIES], 0.0), axis=1, keepdims=True)
    blob_col[...] = jnp.broadcast_to(column, (PITCH, BODIES))
    occupancy[...] = jnp.where(iota((CELLS, BODIES), 0) == cells_in[...], 1.0, 0.0).astype(BF16)
    own_charges = charges(moments_of(state_r))
    copies = start_core(0, own_charges)

    loads["angles"].wait()
    for target, row in enumerate(frame(angles_in[...])):
        for source, value in enumerate(row):
            rotation[3 * target + source : 3 * target + source + 1, :] = value
    copies = start_plane(0, summed(copies, stage_c, 0))
    loads["self"].wait()
    write_operator(self_in, self_op)

    for name in ("perm", "interp", "sibling", "root"):
        loads[name].wait()
    lane_few = iota((8, 512), 1)
    blob_first = blob_row[...]
    blob_rows[...] = jnp.zeros_like(blob_rows)
    for c in range(3):
        blob_rows[c : c + 1, :] = pltpu.roll(blob_first, c * PITCH, axis=1)[0:1] if c else blob_first[0:1]
    perm_row[...] = jnp.full_like(perm_row, -1.0)
    for level in range(2):
        perm = perm_in[level : level + 1, :].astype(F32)
        perm_row[level : level + 1, : 2 * SKEL] = jnp.where(perm >= SKEL, perm + (CELLS - SKEL), perm)
    perm_all = perm_row[...]
    kept_rows = jnp.where(lane_few < SKEL, perm_all, -1.0)[:, :CELLS]
    rest_rows = jnp.where(lane_few < SKEL, pltpu.roll(perm_all, 512 - SKEL, axis=1), -1.0)[:, :CELLS]
    square[...] = jnp.zeros_like(square)
    place = iota((2 * CELLS, CELLS), 0).astype(F32)
    ups = []
    for level in range(2):
        kept = jnp.where(place == kept_rows[level : level + 1], 1.0, 0.0)
        rest = jnp.where(place == rest_rows[level : level + 1], 1.0, 0.0).astype(BF16)
        square[:SKEL, :SKEL] = interp_in[level]
        high, low = split(square[...])
        ups.append(kept + (mm(rest, high) + mm(rest, low)))
        square[:SKEL, :SKEL] = sibling_in[level]
        sibling_op[level, 0], sibling_op[level, 1] = split(square[...])
    up_op[0], up_op[1] = split(ups[0])
    down_op[0], down_op[1] = split(pick(low_bit, ups[0][CELLS:], ups[0][:CELLS]))
    square[:SKEL, :SKEL] = root_in[...]
    below = mm3(split(square[...]), split(pick(high_bit, ups[1][CELLS:], ups[1][:CELLS])), NT)
    root_op[0], root_op[1] = split(mm3(split(ups[1]), split(below)))

    forward_halo(0, 2 - odd)
    copies = start_far(0, copies, own_charges)
    write_self(state_r, state_u)
    forward_halo(0, 1 + odd)

    loads["near"].wait()
    write_operator(near_in, near_op)
    write_own_gather(state_r)
    wait_boxes(0, (0, 3))
    own_gather[...] = add_boxes(0, 0, 4)
    near = pair(near_op)
    near_moments = stacked(mm_few(blob_rows[...], near))
    self_moments = moments_of(state_u)
    self_rim[...] = state_u[:, :128].T[:RIM]
    values = far_values(0, copies)
    columns = jnp.concatenate([values, jnp.zeros((120, BODIES), F32)], axis=0)[:, :128].T[:RIM]
    self_rim[...] += sum(columns[:, c : c + 1] * blob_rows[c : c + 1, :] for c in range(3))
    add_far(state_u, values)
    drain()
    wait_boxes(0, (4, 5, 6, 7))

    high, low = split(add_boxes(0, 4, 8))
    rim[1] = self_rim[...] + mm3((high[:RIM], low[:RIM]), near, NT)
    start_halo(1)
    moments = self_moments + blob_square * values + fold(mm(near_moments, high, NT) + mm(near_moments, low, NT))
    own_charges = charges(moments)
    copies = start_core(1, own_charges)
    state_u[...] += mm3(near, (high, low), NT)
    copies = start_plane(1, summed(copies, stage_c, 1))
    write_self(state_u, state_t)
    write_own_gather(state_u)
    forward_halo(1, 2 - odd)
    for c in range(3):
        u_out[c] = state_u[body_rows(c), :]

    tiny = 1e-30
    rr = total(state_r[...] * state_r[...])
    ru = total(state_r[...] * state_u[...])
    over_rr = jnp.where(rr > 0.0, 1.0 / jnp.where(rr > 0.0, rr, 1.0), 0.0)
    forward_halo(1, 1 + odd)
    copies = start_far(1, copies, own_charges)
    state_u[...] = state_u[...] - (ru * over_rr) * state_r[...]
    uu = total(state_u[...] * state_u[...])
    over_uu = jnp.where(uu > 0.0, 1.0 / jnp.where(uu > 0.0, uu, 1.0), 0.0)
    wait_boxes(1, (0, 3))
    own_gather[...] = add_boxes(1, 0, 4)
    drain()

    add_far(state_t, far_values(1, copies))
    wait_boxes(1, (4, 5, 6, 7))
    state_t[...] += mm3(near, split(add_boxes(1, 4, 8)), NT)

    largest = jnp.maximum(jnp.max(jnp.abs(state_t[...]), axis=(0, 1), keepdims=True), tiny)
    scaled = state_t[...] * (1.0 / largest)
    state_t[...] = scaled
    rt = total(state_r[...] * scaled)
    ut = total(state_u[...] * scaled)
    state_t[...] = state_t[...] - (rt * over_rr) * state_r[...] - (ut * over_uu) * state_u[...]
    tt = total(state_t[...] * state_t[...])
    root_rr, root_uu = jnp.sqrt(rr), jnp.sqrt(uu)
    triangle = [
        root_rr,
        ru * over_rr * root_rr,
        root_uu,
        largest * (rt * over_rr * root_rr),
        largest * (ut * over_uu * root_uu),
        largest * jnp.sqrt(tt),
    ]
    row_of = iota((8, 256), 0)
    lane_is_mine = iota((8, 256), 1) == ix + 8 * (iy + 8 * iz)
    tile = jnp.zeros((8, 256), F32)
    for i, value in enumerate(triangle):
        tile = jnp.where((row_of == i) & lane_is_mine, value, tile)
    copies = start_core(2, tile)
    copies = start_plane(2, summed(copies, stage_c, 2))
    copies = start_depth(2, summed(copies, stage_p, 2))
    drain()
    everyone = summed(copies, stage_d, 2)

    r1, u1, u2, t1, t2, t3 = (everyone[i : i + 1] for i in range(6))
    dot = lambda *pairs: total(sum(a * b for a, b in pairs))
    beta = jnp.sqrt(dot((r1, r1)) + epsilon)
    v1 = r1 / beta
    image1, image2 = v1 + u1 / beta, u2 / beta
    diag_first = dot((image1, v1))
    w1, w2 = image1 - diag_first * v1, image2
    below_first = jnp.sqrt(dot((w1, w1), (w2, w2)) + epsilon)
    second1, second2 = w1 / below_first, w2 / below_first
    rest = (1.0 - diag_first) / beta
    z1 = second1 + (t1 / beta + rest * u1) / below_first
    z2 = second2 + (t2 / beta + rest * u2) / below_first
    z3 = (t3 / beta) / below_first
    above_second = dot((z1, v1))
    diag_second = dot((z1, second1), (z2, second2))
    left1 = z1 - above_second * v1 - diag_second * second1
    left2 = z2 - diag_second * second2
    below_second = jnp.sqrt(dot((left1, left1), (left2, left2), (z3, z3)) + epsilon)
    coef_one, coef_two, residual = least_squares(beta, diag_first, below_first, above_second, diag_second, below_second)
    on_r = coef_one / beta + coef_two * rest / below_first
    on_u = coef_two / (below_first * beta)
    for c in range(3):
        u_out[c] = on_r * rhs_in[c] + on_u * u_out[c]
    store = pltpu.make_async_copy(u_out, result_hbm.at[:, :, 0, :], out_sem)
    store.start()
    residual_ref[...] = residual

    store.wait()


def body(rhs, angles, self_mob, near_mat, near_weight, neighbours, cells, blob_weight, skel_perm, interp, sibling_ops, root_op):
    initial = rhs.reshape(3, BLOBS, 1, BODIES)
    operands = [
        initial,
        angles.reshape(3, 1, BODIES),
        self_mob,
        near_mat,
        near_weight.reshape(NEIGH, BODIES),
        neighbours.reshape(NEIGH, BODIES),
        cells.reshape(1, BODIES),
        blob_weight.reshape(1, BLOBS),
        skel_perm,
        interp,
        sibling_ops,
        root_op,
    ]
    vmem = pltpu.VMEM
    dma = pltpu.SemaphoreType.DMA
    result, residual = pl.pallas_call(
        kernel,
        out_shape=(
            jax.ShapeDtypeStruct(initial.shape, F32),
            jax.ShapeDtypeStruct((1, 1), F32),
        ),
        in_specs=[pl.BlockSpec(memory_space=pltpu.HBM)] * len(operands),
        out_specs=(
            pl.BlockSpec(memory_space=pltpu.HBM),
            pl.BlockSpec(memory_space=pltpu.VMEM),
        ),
        scratch_shapes=[vmem((3, BLOBS, BODIES), F32), vmem((3, BODIES), F32)]
        + [vmem(x.shape, x.dtype) for x in operands[2:]]
        + [
            vmem((ROWS, BODIES), F32),
            vmem((ROWS, BODIES), F32),
            vmem((ROWS, BODIES), F32),
            vmem((ROWS, ROWS), F32),
            vmem((2, ROWS, ROWS), BF16),
            vmem((2, ROWS, ROWS), BF16),
            vmem((2, BODIES, BODIES + NEIGH * RIM), BF16),
            vmem((BODIES, 128), F32),
            vmem((128, BODIES), F32),
            vmem((CELLS, BODIES), BF16),
            vmem((8, ROWS), F32),
            vmem((8, ROWS), F32),
            vmem((PITCH, BODIES), F32),
            vmem((16, BODIES), F32),
            vmem((8, 512), F32),
            vmem((CELLS, CELLS), F32),
            vmem((2, 2 * CELLS, CELLS), BF16),
            vmem((2, CELLS, CELLS), BF16),
            vmem((2, 2, CELLS, CELLS), BF16),
            vmem((2, 2 * CELLS, CELLS), BF16),
            vmem((BODIES, ROWS), F32),
            vmem((RIM, ROWS), F32),
            vmem((3, BLOBS, BODIES), F32),
            vmem((2, RIM, ROWS), F32),
            vmem((2, NEIGH, RIM, ROWS), F32),
            vmem((3, len(CORE) + 1, 8, 256), F32),
            vmem((3, len(PLANE) + 1, 8, 256), F32),
            vmem((3, len(DEPTH) + 1, 8, 256), F32),
            dma((len(operands),)),
            dma(()),
            dma((2, NEIGH, PARTS)),
            dma((2, NEIGH, PARTS)),
            dma((3, len(CORE))),
            dma((3, len(CORE))),
            dma((3, len(PLANE))),
            dma((3, len(PLANE))),
            dma((3, len(DEPTH))),
            dma((3, len(DEPTH))),
        ],
        compiler_params=pltpu.CompilerParams(collective_id=0, has_side_effects=True, vmem_limit_bytes=64 * 2**20),
    )(*operands)
    return (result.reshape(rhs.shape), residual.reshape(()))


def solution(mesh):
    in_specs = (
        P("gx", "gy", None, None, "gz"),
        P("gx", "gy", None, "gz"),
        P(),
        P(),
        P("gx", "gy", None, "gz"),
        P("gx", "gy", None, "gz"),
        P("gx", "gy", "gz"),
        P(),
        P(),
        P(),
        P(),
        P(),
    )
    out_specs = (P("gx", "gy", None, None, "gz"), P())
    return jax.shard_map(body, mesh=mesh, in_specs=in_specs, out_specs=out_specs, check_vma=False)
```

```python
import jax
import jax.numpy as jnp
from jax import lax
from jax.experimental import pallas as pl
from jax.experimental.pallas import tpu as pltpu
from jax.sharding import PartitionSpec as P

F32 = jnp.float32
BF16 = jnp.bfloat16
MESH = pl.DeviceIdType.MESH
epsilon = 1e-06

BLOBS = 162
PITCH = 168
ROWS = 512
BODIES = 256
SKEL = 192
CELLS = 256
RIM = 64
NEIGH = 8
NN = (((1,), (0,)), ((), ()))
NT = (((1,), (1,)), ((), ()))
PARTS = 2
PLACES = {1: 0, 3: 1, 5: 2, 7: 3, 0: 4, 2: 5, 6: 6, 8: 7}


def split(x):
    high = x.astype(BF16)
    return high, (x - high.astype(F32)).astype(BF16)


def mm(a, b, dims=NN):
    return lax.dot_general(a, b, dims, preferred_element_type=F32)


def mm3(a, b, dims=NN):
    return mm(a[0], b[0], dims) + (mm(a[0], b[1], dims) + mm(a[1], b[0], dims))


def stacked(x):
    high = x.astype(BF16).astype(F32)
    return jnp.concatenate([high, x - high], axis=0).astype(BF16)


def fold(x):
    half = x.shape[0] // 2
    return x[:half] + x[half:]


def mm_few(x, weights, dims=NN):
    both = stacked(x)
    return fold(mm(both, weights[0], dims) + mm(both, weights[1], dims))


def total(x):
    return jnp.sum(x, axis=(0, 1), keepdims=True)


def iota(shape, dim):
    return lax.broadcasted_iota(jnp.int32, shape, dim)


def frame(angles):
    cos_all, sin_all = jnp.cos(angles), jnp.sin(angles)
    cy, cp, cr = cos_all[0:1], cos_all[1:2], cos_all[2:3]
    sy, sp, sr = sin_all[0:1], sin_all[1:2], sin_all[2:3]
    return (
        (cy * cp, cy * sp * sr - sy * cr, cy * sp * cr + sy * sr),
        (sy * cp, sy * sp * sr + cy * cr, sy * sp * cr - cy * sr),
        (-sp, cp * sr, cp * cr),
    )


def least_squares(beta, diag_first, below_first, above_second, diag_second, below_second):
    first_norm = jnp.sqrt(diag_first * diag_first + below_first * below_first)
    first_cos = diag_first / first_norm
    first_sin = below_first / first_norm
    top_right = first_cos * above_second + first_sin * diag_second
    lower_right = first_cos * diag_second - first_sin * above_second
    second_norm = jnp.sqrt(lower_right * lower_right + below_second * below_second)
    second_cos = lower_right / second_norm
    second_sin = below_second / second_norm
    carried = -first_sin * beta
    coef_two = second_cos * carried / second_norm
    coef_one = (first_cos * beta - top_right * coef_two) / first_norm
    return (coef_one, coef_two, jnp.abs(second_sin * carried))


CORE = [(0, 1, 0, 0, 0)]
PLANE = [(y, 0, x, 0, 0) for y in range(4) for x in range(4) if x or y]
DEPTH = [(0, 0, 0, low, high) for low in range(2) for high in range(4) if low or high]


def ring(step, size):
    return min(step % size, -step % size)


def hops(offset):
    y, _, x, low, high = offset
    return ring(y, 4) + ring(x, 4) + ring(2 * high + low, 8)


def kernel(
    rhs_hbm, angles_hbm, self_hbm, near_hbm, weight_hbm, links_hbm, cells_hbm, blob_hbm, perm_hbm, interp_hbm, sibling_hbm, root_hbm,
    result_hbm, residual_ref,
    rhs_in, angles_in, self_in, near_in, weight_in, links_in, cells_in, blob_in, perm_in, interp_in, sibling_in, root_in,
    state_r, state_u, state_t, padded_mat, self_op, near_op, link_op, link_cols, link_rows, occupancy, blob_row, blob_rows, blob_col,
    rotation, perm_row, square, up_op, down_op, sibling_op, root_op, own_gather, self_rim, u_out,
    rim, halo, stage_c, stage_p, stage_d,
    in_sem, out_sem, rim_send, rim_recv, c_send, c_recv, p_send, p_recv, d_send, d_recv,
):
    ix, iy, iz = lax.axis_index("gx"), lax.axis_index("gy"), lax.axis_index("gz")
    pending = []

    def body_rows(c):
        return slice(c * PITCH, c * PITCH + BLOBS)

    def pad_rows(c):
        return slice(c * PITCH + BLOBS, (c + 1) * PITCH if c < 2 else ROWS)

    for c in range(3):
        state_r[pad_rows(c), :] = jnp.zeros_like(state_r[pad_rows(c), :])
    pairs = {
        "rhs": (rhs_hbm.at[:, :, 0, :128], rhs_in.at[:, :, :128]),
        "rest": (rhs_hbm.at[:, :, 0, 128:], rhs_in.at[:, :, 128:]),
        "blob": (blob_hbm, blob_in),
        "cells": (cells_hbm, cells_in),
        "angles": (angles_hbm.at[:, 0, :], angles_in),
        "self": (self_hbm, self_in),
        "weight": (weight_hbm, weight_in),
        "links": (links_hbm, links_in),
        "perm": (perm_hbm, perm_in),
        "interp": (interp_hbm, interp_in),
        "sibling": (sibling_hbm, sibling_in),
        "root": (root_hbm, root_in),
        "near": (near_hbm, near_in),
    }
    loads = {name: pltpu.make_async_copy(a, b, in_sem.at[i]) for i, (name, (a, b)) in enumerate(pairs.items())}
    loads["rhs"].start()

    def wrapped(index, shift, size):
        return lax.rem(index + shift + size, size)

    odd = lax.rem(iy, 2)
    plus, minus = {"gx": wrapped(ix, 1, 8)}, {"gx": wrapped(ix, -1, 8)}
    across = {"gy": wrapped(iy, 2 * odd - 1, 8)}
    beside = {"gy": iy + 1 - 2 * odd}
    far_gx = {"gx": wrapped(ix, 2 * lax.rem(ix, 2) - 1, 8)}

    known = {}

    def peer(offset):
        if offset not in known:
            known[offset] = device_at(offset)
        return known[offset]

    def device_at(offset):
        y, core, x, low, high = offset
        device = {}
        if y or core:
            device["gx"] = 2 * lax.rem(ix // 2 + y, 4) + lax.rem(ix + core, 2)
        if x or low:
            device["gy"] = 2 * lax.rem(iy // 2 + x, 4) + lax.rem(iy + low, 2)
        if high:
            device["gz"] = iz ^ high
        return device

    barrier = pltpu.get_barrier_semaphore()
    greeted = [across, far_gx] + [peer(o) for o in sorted(DEPTH + PLANE + CORE, key=hops, reverse=True)]
    for device in greeted:
        pl.semaphore_signal(barrier, inc=1, device_id=device, device_id_type=MESH)
    for name, load in loads.items():
        if name != "rhs":
            load.start()

    def remote(src, dst, send_sem, recv_sem, device):
        return pltpu.make_async_remote_copy(
            src_ref=src, dst_ref=dst, send_sem=send_sem, recv_sem=recv_sem, device_id=device, device_id_type=MESH
        )

    def send(*what):
        copy = remote(*what)
        copy.start()
        pending.append(copy)
        return copy

    def drain():
        for copy in pending:
            copy.wait_send()
        pending.clear()

    part = RIM // PARTS

    def box_copy(phase, source, place, i, device):
        rows = pl.ds(i * part, part)
        return (source.at[rows], halo.at[phase, place, rows], rim_send.at[phase, place, i], rim_recv.at[phase, place, i], device)

    def start_halo(phase):
        own = rim.at[phase]
        for i in range(PARTS):
            send(*box_copy(phase, own, 1 + odd, i, beside))
        for i in range(PARTS):
            send(*box_copy(phase, own, 2 - odd, i, across))
        for i in range(PARTS):
            send(*box_copy(phase, own, 0, i, plus))
            send(*box_copy(phase, own, 3, i, minus))

    def forward_halo(phase, place):
        box = halo.at[phase, place]
        for i in range(PARTS):
            remote(*box_copy(phase, rim.at[phase], place, i, plus)).wait_recv()
            send(*box_copy(phase, box, place + 3, i, plus))
            send(*box_copy(phase, box, place + 5, i, minus))

    def wait_boxes(phase, places):
        for place in places:
            for i in range(PARTS):
                remote(*box_copy(phase, rim.at[phase], place, i, plus)).wait_recv()

    def exchange(stage, send_sem, recv_sem, group, turn, value):
        stage[turn, 0] = value
        order = sorted(range(len(group)), key=lambda i: -hops(group[i]))
        copies = [
            send(stage.at[turn, 0], stage.at[turn, i + 1], send_sem.at[turn, i], recv_sem.at[turn, i], peer(group[i])) for i in order
        ]
        return copies[::-1]

    def packed(x):
        return x[:, :128] + pltpu.roll(x[:, 128:], 3, axis=0)

    def unpacked(x):
        top = iota((8, 128), 0) < 3
        return jnp.concatenate([jnp.where(top, x, 0.0), jnp.where(top, pltpu.roll(x, 5, axis=0), 0.0)], axis=1)

    def start_core(turn, value):
        return exchange(stage_c, c_send, c_recv, CORE, turn, value)

    def start_plane(turn, value):
        return exchange(stage_p, p_send, p_recv, PLANE, turn, value)

    def start_depth(turn, value):
        return exchange(stage_d, d_send, d_recv, DEPTH, turn, value)

    def summed(copies, stage, turn):
        for copy in copies:
            copy.wait_recv()
        return jnp.sum(stage[turn], axis=0)

    def start_far(turn, copies, own):
        return start_depth(turn, unpacked(summed(copies, stage_p, turn)) + pltpu.roll(own, 3, axis=0))

    def moments_of(state):
        rows = [
            jnp.sum(blob_col[...] * state[c * PITCH : (c + 1) * PITCH, :], axis=0, keepdims=True) for c in range(3)
        ]
        return jnp.concatenate(rows + [jnp.zeros((5, BODIES), F32)], axis=0)

    def charges(moments):
        return fold(mm(stacked(moments), occupancy[...], NT))

    low_bit = lax.rem(iz, 2) == 1
    high_bit = iz // 2 == 1

    def pick(flag, a, b):
        return jnp.where(flag, a, b)

    def pair(ref):
        return (ref[0], ref[1])

    def far_values(turn, copies):
        for copy in copies:
            copy.wait_recv()
        top = iota((8, CELLS), 0) < 3
        layers = []
        for high in range(4):
            here = stage_d[turn, DEPTH.index((0, 0, 0, 0, high)) + 1 if high else 0]
            there = stage_d[turn, DEPTH.index((0, 0, 0, 1, high)) + 1]
            layers.append(jnp.where(top, here + there - pltpu.roll(here, 5, axis=0), here))
        own, one, two, three = layers
        joined = jnp.concatenate(
            [
                jnp.concatenate([pick(low_bit, one, own), pick(low_bit, own, one)], axis=1),
                jnp.concatenate([pick(low_bit, three, two), pick(low_bit, two, three)], axis=1),
            ],
            axis=0,
        )
        first = mm_few(joined, pair(up_op))
        mine, partner = first[:8], first[8:]
        second = jnp.concatenate([pick(high_bit, partner, mine), pick(high_bit, mine, partner)], axis=1)
        potential = mm_few(second, pair(root_op)) + pltpu.roll(mm_few(partner, pair(sibling_op.at[1])), 5, axis=0)
        potential = mm_few(potential, pair(down_op), NT) + pltpu.roll(mm_few(one, pair(sibling_op.at[0])), 5, axis=0)
        return jnp.where(top, fold(mm(stacked(potential), occupancy[...])), 0.0)

    def factor(target, source, inverse):
        index = 3 * source + target if inverse else 3 * target + source
        return rotation[index : index + 1, :]

    def rotated(parts, inverse):
        return [
            factor(target, 0, inverse) * parts[0] + factor(target, 1, inverse) * parts[1] + factor(target, 2, inverse) * parts[2]
            for target in range(3)
        ]

    def write_self(state, result):
        parts = [state[c * PITCH : (c + 1) * PITCH, :] for c in range(3)]
        turned = jnp.concatenate(rotated(parts, False) + [jnp.zeros((ROWS - 3 * PITCH, BODIES), F32)], axis=0)
        mixture = mm3((self_op[0], self_op[1]), split(turned))
        back = rotated([mixture[c * PITCH : (c + 1) * PITCH] for c in range(3)], True)
        for c in range(3):
            result[c * PITCH : (c + 1) * PITCH, :] = back[c]
        result[3 * PITCH :, :] = jnp.zeros((ROWS - 3 * PITCH, BODIES), F32)

    def write_own_gather(state):
        own_gather[...] = mm3((link_op[0, :, :BODIES], link_op[1, :, :BODIES]), split(state[...]), NT)

    def add_boxes(phase, first, last):
        lanes = slice(BODIES + first * RIM, BODIES + last * RIM)
        boxes = split(halo[phase, first:last].reshape((last - first) * RIM, ROWS))
        return own_gather[...] + mm3((link_op[0, :, lanes], link_op[1, :, lanes]), boxes)

    def add_far(result, values):
        for c in range(3):
            result[c * PITCH : (c + 1) * PITCH, :] += blob_col[...] * values[c : c + 1, :]

    def write_operator(source, target):
        padded_mat[...] = jnp.zeros_like(padded_mat)
        for c in range(3):
            padded_mat[c * PITCH : c * PITCH + BLOBS, : 3 * BLOBS] = source[c * BLOBS : (c + 1) * BLOBS, :]
        matrix = padded_mat[...]
        lane = iota((ROWS, ROWS), 1)
        gap = PITCH - BLOBS
        spread = jnp.where(
            lane < PITCH, matrix, jnp.where(lane < 2 * PITCH, pltpu.roll(matrix, gap, axis=1), pltpu.roll(matrix, 2 * gap, axis=1))
        )
        target[0], target[1] = split(spread)

    loads["rhs"].wait()
    for c in range(3):
        state_r[body_rows(c), :128] = rhs_in[c, :, :128]
    rim[0] = state_r[:, :128].T[:RIM]
    loads["rest"].wait()
    for c in range(3):
        state_r[body_rows(c), 128:] = rhs_in[c, :, 128:]
    loads["weight"].wait()
    loads["links"].wait()
    links = links_in[...]
    box, body = links // BODIES, lax.rem(links, BODIES)
    place = jnp.zeros_like(box)
    for slot, index in PLACES.items():
        place = jnp.where(box == slot, index, place)
    lane_of = jnp.where(box == 4, body, BODIES + place * RIM + body)
    link_rows[...] = jnp.zeros_like(link_rows)
    link_rows[0:NEIGH, :] = lane_of.astype(F32)
    link_rows[NEIGH : 2 * NEIGH, :] = weight_in[...]
    link_cols[...] = link_rows[...].T
    block = 32

    @pl.loop(0, BODIES // block)
    def _(i):
        rows = pl.ds(pl.multiple_of(i * block, block), block)
        entries = link_cols[rows, :]
        width = BODIES + NEIGH * RIM
        lane = iota((block, width), 1).astype(F32)
        weights = jnp.zeros((block, width), F32)
        for k in range(NEIGH):
            weights = weights + jnp.where(lane == entries[:, k : k + 1], entries[:, NEIGH + k : NEIGH + k + 1], 0.0)
        link_op[0, rows, :], link_op[1, rows, :] = split(weights)

    pl.semaphore_wait(barrier, len(greeted))
    start_halo(0)

    loads["blob"].wait()
    loads["cells"].wait()
    blob_row[...] = jnp.zeros_like(blob_row)
    blob_row[0:1, :BLOBS] = blob_in[...]
    diagonal = iota((PITCH, BODIES), 0) == iota((PITCH, BODIES), 1)
    blob_square = total(blob_row[0:1, :] * blob_row[0:1, :])
    column = jnp.sum(jnp.where(diagonal, blob_row[0:1, :BODIES], 0.0), axis=1, keepdims=True)
    blob_col[...] = jnp.broadcast_to(column, (PITCH, BODIES))
    occupancy[...] = jnp.where(iota((CELLS, BODIES), 0) == cells_in[...], 1.0, 0.0).astype(BF16)
    own_charges = charges(moments_of(state_r))
    copies = start_core(0, packed(own_charges))

    loads["angles"].wait()
    for target, row in enumerate(frame(angles_in[...])):
        for source, value in enumerate(row):
            rotation[3 * target + source : 3 * target + source + 1, :] = value
    copies = start_plane(0, summed(copies, stage_c, 0))
    loads["self"].wait()
    write_operator(self_in, self_op)

    for name in ("perm", "interp", "sibling", "root"):
        loads[name].wait()
    lane_few = iota((8, 512), 1)
    blob_first = blob_row[...]
    blob_rows[...] = jnp.zeros_like(blob_rows)
    for c in range(3):
        blob_rows[c : c + 1, :] = pltpu.roll(blob_first, c * PITCH, axis=1)[0:1] if c else blob_first[0:1]
    perm_row[...] = jnp.full_like(perm_row, -1.0)
    for level in range(2):
        perm = perm_in[level : level + 1, :].astype(F32)
        perm_row[level : level + 1, : 2 * SKEL] = jnp.where(perm >= SKEL, perm + (CELLS - SKEL), perm)
    perm_all = perm_row[...]
    kept_rows = jnp.where(lane_few < SKEL, perm_all, -1.0)[:, :CELLS]
    rest_rows = jnp.where(lane_few < SKEL, pltpu.roll(perm_all, 512 - SKEL, axis=1), -1.0)[:, :CELLS]
    square[...] = jnp.zeros_like(square)
    place = iota((2 * CELLS, CELLS), 0).astype(F32)
    ups = []
    for level in range(2):
        kept = jnp.where(place == kept_rows[level : level + 1], 1.0, 0.0)
        rest = jnp.where(place == rest_rows[level : level + 1], 1.0, 0.0).astype(BF16)
        square[:SKEL, :SKEL] = interp_in[level]
        high, low = split(square[...])
        ups.append(kept + (mm(rest, high) + mm(rest, low)))
        square[:SKEL, :SKEL] = sibling_in[level]
        sibling_op[level, 0], sibling_op[level, 1] = split(square[...])
    up_op[0], up_op[1] = split(ups[0])
    down_op[0], down_op[1] = split(pick(low_bit, ups[0][CELLS:], ups[0][:CELLS]))
    square[:SKEL, :SKEL] = root_in[...]
    below = mm3(split(square[...]), split(pick(high_bit, ups[1][CELLS:], ups[1][:CELLS])), NT)
    root_op[0], root_op[1] = split(mm3(split(ups[1]), split(below)))

    forward_halo(0, 2 - odd)
    copies = start_far(0, copies, own_charges)
    write_self(state_r, state_u)
    forward_halo(0, 1 + odd)

    loads["near"].wait()
    write_operator(near_in, near_op)
    write_own_gather(state_r)
    wait_boxes(0, (0, 3))
    own_gather[...] = add_boxes(0, 0, 4)
    near = pair(near_op)
    near_moments = stacked(mm_few(blob_rows[...], near))
    self_moments = moments_of(state_u)
    self_rim[...] = state_u[:, :128].T[:RIM]
    values = far_values(0, copies)
    columns = jnp.concatenate([values, jnp.zeros((120, BODIES), F32)], axis=0)[:, :128].T[:RIM]
    self_rim[...] += sum(columns[:, c : c + 1] * blob_rows[c : c + 1, :] for c in range(3))
    add_far(state_u, values)
    drain()
    wait_boxes(0, (4, 5, 6, 7))

    high, low = split(add_boxes(0, 4, 8))
    moments = self_moments + blob_square * values + fold(mm(near_moments, high, NT) + mm(near_moments, low, NT))
    own_charges = charges(moments)
    copies = start_core(1, packed(own_charges))
    rim[1] = self_rim[...] + mm3((high[:RIM], low[:RIM]), near, NT)
    start_halo(1)
    state_u[...] += mm3(near, (high, low), NT)
    copies = start_plane(1, summed(copies, stage_c, 1))
    write_self(state_u, state_t)
    write_own_gather(state_u)
    forward_halo(1, 2 - odd)
    for c in range(3):
        u_out[c] = state_u[body_rows(c), :]

    tiny = 1e-30
    rr = total(state_r[...] * state_r[...])
    ru = total(state_r[...] * state_u[...])
    over_rr = jnp.where(rr > 0.0, 1.0 / jnp.where(rr > 0.0, rr, 1.0), 0.0)
    copies = start_far(1, copies, own_charges)
    forward_halo(1, 1 + odd)
    state_u[...] = state_u[...] - (ru * over_rr) * state_r[...]
    uu = total(state_u[...] * state_u[...])
    over_uu = jnp.where(uu > 0.0, 1.0 / jnp.where(uu > 0.0, uu, 1.0), 0.0)
    wait_boxes(1, (0, 3))
    own_gather[...] = add_boxes(1, 0, 4)
    drain()

    add_far(state_t, far_values(1, copies))
    wait_boxes(1, (4, 5, 6, 7))
    state_t[...] += mm3(near, split(add_boxes(1, 4, 8)), NT)

    largest = jnp.maximum(jnp.max(jnp.abs(state_t[...]), axis=(0, 1), keepdims=True), tiny)
    scaled = state_t[...] * (1.0 / largest)
    state_t[...] = scaled
    rt = total(state_r[...] * scaled)
    ut = total(state_u[...] * scaled)
    state_t[...] = state_t[...] - (rt * over_rr) * state_r[...] - (ut * over_uu) * state_u[...]
    tt = total(state_t[...] * state_t[...])
    root_rr, root_uu = jnp.sqrt(rr), jnp.sqrt(uu)
    triangle = [
        root_rr,
        ru * over_rr * root_rr,
        root_uu,
        largest * (rt * over_rr * root_rr),
        largest * (ut * over_uu * root_uu),
        largest * jnp.sqrt(tt),
    ]
    height = 2 * iz + odd
    row_of = iota((8, 128), 0)
    lane_is_mine = iota((8, 128), 1) == 4 * ix + iy // 2 + 32 * lax.rem(height, 4)
    tile = jnp.zeros((8, 128), F32)
    for i, value in enumerate(triangle):
        tile = jnp.where((row_of == i) & lane_is_mine, value, tile)
    copies = start_core(2, tile)
    copies = start_plane(2, summed(copies, stage_c, 2))
    tile = summed(copies, stage_p, 2)
    copies = start_depth(2, jnp.concatenate([jnp.where(height < 4, tile, 0.0), jnp.where(height < 4, 0.0, tile)], axis=1))
    drain()
    everyone = summed(copies, stage_d, 2)

    r1, u1, u2, t1, t2, t3 = (everyone[i : i + 1] for i in range(6))
    dot = lambda *pairs: total(sum(a * b for a, b in pairs))
    beta = jnp.sqrt(dot((r1, r1)) + epsilon)
    v1 = r1 / beta
    image1, image2 = v1 + u1 / beta, u2 / beta
    diag_first = dot((image1, v1))
    w1, w2 = image1 - diag_first * v1, image2
    below_first = jnp.sqrt(dot((w1, w1), (w2, w2)) + epsilon)
    second1, second2 = w1 / below_first, w2 / below_first
    rest = (1.0 - diag_first) / beta
    z1 = second1 + (t1 / beta + rest * u1) / below_first
    z2 = second2 + (t2 / beta + rest * u2) / below_first
    z3 = (t3 / beta) / below_first
    above_second = dot((z1, v1))
    diag_second = dot((z1, second1), (z2, second2))
    left1 = z1 - above_second * v1 - diag_second * second1
    left2 = z2 - diag_second * second2
    below_second = jnp.sqrt(dot((left1, left1), (left2, left2), (z3, z3)) + epsilon)
    coef_one, coef_two, residual = least_squares(beta, diag_first, below_first, above_second, diag_second, below_second)
    on_r = coef_one / beta + coef_two * rest / below_first
    on_u = coef_two / (below_first * beta)
    for c in range(3):
        u_out[c] = on_r * rhs_in[c] + on_u * u_out[c]
    store = pltpu.make_async_copy(u_out, result_hbm.at[:, :, 0, :], out_sem)
    store.start()
    residual_ref[...] = residual

    store.wait()


def body(rhs, angles, self_mob, near_mat, near_weight, neighbours, cells, blob_weight, skel_perm, interp, sibling_ops, root_op):
    initial = rhs.reshape(3, BLOBS, 1, BODIES)
    operands = [
        initial,
        angles.reshape(3, 1, BODIES),
        self_mob,
        near_mat,
        near_weight.reshape(NEIGH, BODIES),
        neighbours.reshape(NEIGH, BODIES),
        cells.reshape(1, BODIES),
        blob_weight.reshape(1, BLOBS),
        skel_perm,
        interp,
        sibling_ops,
        root_op,
    ]
    vmem = pltpu.VMEM
    dma = pltpu.SemaphoreType.DMA
    result, residual = pl.pallas_call(
        kernel,
        out_shape=(
            jax.ShapeDtypeStruct(initial.shape, F32),
            jax.ShapeDtypeStruct((1, 1), F32),
        ),
        in_specs=[pl.BlockSpec(memory_space=pltpu.HBM)] * len(operands),
        out_specs=(
            pl.BlockSpec(memory_space=pltpu.HBM),
            pl.BlockSpec(memory_space=pltpu.VMEM),
        ),
        scratch_shapes=[vmem((3, BLOBS, BODIES), F32), vmem((3, BODIES), F32)]
        + [vmem(x.shape, x.dtype) for x in operands[2:]]
        + [
            vmem((ROWS, BODIES), F32),
            vmem((ROWS, BODIES), F32),
            vmem((ROWS, BODIES), F32),
            vmem((ROWS, ROWS), F32),
            vmem((2, ROWS, ROWS), BF16),
            vmem((2, ROWS, ROWS), BF16),
            vmem((2, BODIES, BODIES + NEIGH * RIM), BF16),
            vmem((BODIES, 128), F32),
            vmem((128, BODIES), F32),
            vmem((CELLS, BODIES), BF16),
            vmem((8, ROWS), F32),
            vmem((8, ROWS), F32),
            vmem((PITCH, BODIES), F32),
            vmem((16, BODIES), F32),
            vmem((8, 512), F32),
            vmem((CELLS, CELLS), F32),
            vmem((2, 2 * CELLS, CELLS), BF16),
            vmem((2, CELLS, CELLS), BF16),
            vmem((2, 2, CELLS, CELLS), BF16),
            vmem((2, 2 * CELLS, CELLS), BF16),
            vmem((BODIES, ROWS), F32),
            vmem((RIM, ROWS), F32),
            vmem((3, BLOBS, BODIES), F32),
            vmem((2, RIM, ROWS), F32),
            vmem((2, NEIGH, RIM, ROWS), F32),
            vmem((3, len(CORE) + 1, 8, 128), F32),
            vmem((3, len(PLANE) + 1, 8, 128), F32),
            vmem((3, len(DEPTH) + 1, 8, 256), F32),
            dma((len(operands) + 1,)),
            dma(()),
            dma((2, NEIGH, PARTS)),
            dma((2, NEIGH, PARTS)),
            dma((3, len(CORE))),
            dma((3, len(CORE))),
            dma((3, len(PLANE))),
            dma((3, len(PLANE))),
            dma((3, len(DEPTH))),
            dma((3, len(DEPTH))),
        ],
        compiler_params=pltpu.CompilerParams(collective_id=0, has_side_effects=True, vmem_limit_bytes=64 * 2**20),
    )(*operands)
    return (result.reshape(rhs.shape), residual.reshape(()))


def solution(mesh):
    in_specs = (
        P("gx", "gy", None, None, "gz"),
        P("gx", "gy", None, "gz"),
        P(),
        P(),
        P("gx", "gy", None, "gz"),
        P("gx", "gy", None, "gz"),
        P("gx", "gy", "gz"),
        P(),
        P(),
        P(),
        P(),
        P(),
    )
    out_specs = (P("gx", "gy", None, None, "gz"), P())
    return jax.shard_map(body, mesh=mesh, in_specs=in_specs, out_specs=out_specs, check_vma=False)
```

```python
import jax
import jax.numpy as jnp
from jax import lax
from jax.experimental import pallas as pl
from jax.experimental.pallas import tpu as pltpu
from jax.sharding import PartitionSpec as P

F32 = jnp.float32
BF16 = jnp.bfloat16
MESH = pl.DeviceIdType.MESH
epsilon = 1e-06

BLOBS = 162
PITCH = 168
ROWS = 512
BODIES = 256
SKEL = 192
CELLS = 256
RIM = 64
NEIGH = 8
NN = (((1,), (0,)), ((), ()))
NT = (((1,), (1,)), ((), ()))
PARTS = 2
PLACES = {1: 0, 3: 1, 5: 2, 7: 3, 0: 4, 2: 5, 6: 6, 8: 7}


def split(x):
    high = x.astype(BF16)
    return high, (x - high.astype(F32)).astype(BF16)


def mm(a, b, dims=NN):
    return lax.dot_general(a, b, dims, preferred_element_type=F32)


def mm3(a, b, dims=NN):
    return mm(a[0], b[0], dims) + (mm(a[0], b[1], dims) + mm(a[1], b[0], dims))


def stacked(x):
    high = x.astype(BF16).astype(F32)
    return jnp.concatenate([high, x - high], axis=0).astype(BF16)


def fold(x):
    half = x.shape[0] // 2
    return x[:half] + x[half:]


def mm_few(x, weights, dims=NN):
    both = stacked(x)
    return fold(mm(both, weights[0], dims) + mm(both, weights[1], dims))


def total(x):
    return jnp.sum(x, axis=(0, 1), keepdims=True)


def iota(shape, dim):
    return lax.broadcasted_iota(jnp.int32, shape, dim)


def frame(angles):
    cos_all, sin_all = jnp.cos(angles), jnp.sin(angles)
    cy, cp, cr = cos_all[0:1], cos_all[1:2], cos_all[2:3]
    sy, sp, sr = sin_all[0:1], sin_all[1:2], sin_all[2:3]
    return (
        (cy * cp, cy * sp * sr - sy * cr, cy * sp * cr + sy * sr),
        (sy * cp, sy * sp * sr + cy * cr, sy * sp * cr - cy * sr),
        (-sp, cp * sr, cp * cr),
    )


def least_squares(beta, diag_first, below_first, above_second, diag_second, below_second):
    first_norm = jnp.sqrt(diag_first * diag_first + below_first * below_first)
    first_cos = diag_first / first_norm
    first_sin = below_first / first_norm
    top_right = first_cos * above_second + first_sin * diag_second
    lower_right = first_cos * diag_second - first_sin * above_second
    second_norm = jnp.sqrt(lower_right * lower_right + below_second * below_second)
    second_cos = lower_right / second_norm
    second_sin = below_second / second_norm
    carried = -first_sin * beta
    coef_two = second_cos * carried / second_norm
    coef_one = (first_cos * beta - top_right * coef_two) / first_norm
    return (coef_one, coef_two, jnp.abs(second_sin * carried))


CORE = [(0, 1, 0, 0, 0)]
PLANE = [(y, 0, x, 0, 0) for y in range(4) for x in range(4) if x or y]
DEPTH = [(0, 0, 0, low, high) for low in range(2) for high in range(4) if low or high]


def ring(step, size):
    return min(step % size, -step % size)


def hops(offset):
    y, _, x, low, high = offset
    return ring(y, 4) + ring(x, 4) + ring(2 * high + low, 8)


def kernel(
    rhs_hbm, angles_hbm, self_hbm, near_hbm, weight_hbm, links_hbm, cells_hbm, blob_hbm, perm_hbm, interp_hbm, sibling_hbm, root_hbm,
    result_hbm, residual_ref,
    rhs_in, angles_in, self_in, near_in, weight_in, links_in, cells_in, blob_in, perm_in, interp_in, sibling_in, root_in,
    state_r, state_u, state_t, padded_mat, self_op, near_op, link_op, link_cols, link_rows, occupancy, blob_row, blob_rows, blob_col,
    rotation, perm_row, square, up_op, down_op, sibling_op, root_op, own_gather, self_rim, u_out,
    rim, halo, stage_c, stage_p, stage_d,
    in_sem, out_sem, rim_send, rim_recv, c_send, c_recv, p_send, p_recv, d_send, d_recv,
):
    ix, iy, iz = lax.axis_index("gx"), lax.axis_index("gy"), lax.axis_index("gz")
    pending = []

    def body_rows(c):
        return slice(c * PITCH, c * PITCH + BLOBS)

    def pad_rows(c):
        return slice(c * PITCH + BLOBS, (c + 1) * PITCH if c < 2 else ROWS)

    for c in range(3):
        state_r[pad_rows(c), :] = jnp.zeros_like(state_r[pad_rows(c), :])
    pairs = {
        "rhs": (rhs_hbm.at[:, :, 0, :128], rhs_in.at[:, :, :128]),
        "rest": (rhs_hbm.at[:, :, 0, 128:], rhs_in.at[:, :, 128:]),
        "blob": (blob_hbm, blob_in),
        "cells": (cells_hbm, cells_in),
        "angles": (angles_hbm.at[:, 0, :], angles_in),
        "self": (self_hbm, self_in),
        "weight": (weight_hbm, weight_in),
        "links": (links_hbm, links_in),
        "perm": (perm_hbm, perm_in),
        "interp": (interp_hbm, interp_in),
        "sibling": (sibling_hbm, sibling_in),
        "root": (root_hbm, root_in),
        "near": (near_hbm, near_in),
    }
    loads = {name: pltpu.make_async_copy(a, b, in_sem.at[i]) for i, (name, (a, b)) in enumerate(pairs.items())}
    loads["rhs"].start()

    def wrapped(index, shift, size):
        return lax.rem(index + shift + size, size)

    odd = lax.rem(iy, 2)
    plus, minus = {"gx": wrapped(ix, 1, 8)}, {"gx": wrapped(ix, -1, 8)}
    across = {"gy": wrapped(iy, 2 * odd - 1, 8)}
    beside = {"gy": iy + 1 - 2 * odd}
    far_gx = {"gx": wrapped(ix, 2 * lax.rem(ix, 2) - 1, 8)}

    known = {}

    def peer(offset):
        if offset not in known:
            known[offset] = device_at(offset)
        return known[offset]

    def device_at(offset):
        y, core, x, low, high = offset
        device = {}
        if y or core:
            device["gx"] = 2 * lax.rem(ix // 2 + y, 4) + lax.rem(ix + core, 2)
        if x or low:
            device["gy"] = 2 * lax.rem(iy // 2 + x, 4) + lax.rem(iy + low, 2)
        if high:
            device["gz"] = iz ^ high
        return device

    barrier = pltpu.get_barrier_semaphore()
    greeted = [across, far_gx] + [peer(o) for o in sorted(DEPTH + PLANE + CORE, key=hops, reverse=True)]
    for device in greeted:
        pl.semaphore_signal(barrier, inc=1, device_id=device, device_id_type=MESH)
    for name, load in loads.items():
        if name != "rhs":
            load.start()

    def remote(src, dst, send_sem, recv_sem, device):
        return pltpu.make_async_remote_copy(
            src_ref=src, dst_ref=dst, send_sem=send_sem, recv_sem=recv_sem, device_id=device, device_id_type=MESH
        )

    def send(*what):
        copy = remote(*what)
        copy.start()
        pending.append(copy)
        return copy

    def drain():
        for copy in pending:
            copy.wait_send()
        pending.clear()

    part = RIM // PARTS

    def box_copy(phase, source, place, i, device):
        rows = pl.ds(i * part, part)
        return (source.at[rows], halo.at[phase, place, rows], rim_send.at[phase, place, i], rim_recv.at[phase, place, i], device)

    def start_halo(phase):
        own = rim.at[phase]
        for i in range(PARTS):
            send(*box_copy(phase, own, 1 + odd, i, beside))
        for i in range(PARTS):
            send(*box_copy(phase, own, 0, i, plus))
            send(*box_copy(phase, own, 3, i, minus))
        for i in range(PARTS):
            send(*box_copy(phase, own, 2 - odd, i, across))

    def forward_halo(phase, place):
        box = halo.at[phase, place]
        for i in range(PARTS):
            remote(*box_copy(phase, rim.at[phase], place, i, plus)).wait_recv()
            send(*box_copy(phase, box, place + 3, i, plus))
            send(*box_copy(phase, box, place + 5, i, minus))

    def wait_boxes(phase, places):
        for place in places:
            for i in range(PARTS):
                remote(*box_copy(phase, rim.at[phase], place, i, plus)).wait_recv()

    def exchange(stage, send_sem, recv_sem, group, turn, value):
        stage[turn, 0] = value
        order = sorted(range(len(group)), key=lambda i: -hops(group[i]))
        copies = [
            send(stage.at[turn, 0], stage.at[turn, i + 1], send_sem.at[turn, i], recv_sem.at[turn, i], peer(group[i])) for i in order
        ]
        return copies[::-1]

    def packed(x):
        return x[:, :128] + pltpu.roll(x[:, 128:], 3, axis=0)

    def unpacked(x):
        top = iota((8, 128), 0) < 3
        return jnp.concatenate([jnp.where(top, x, 0.0), jnp.where(top, pltpu.roll(x, 5, axis=0), 0.0)], axis=1)

    def start_core(turn, value):
        return exchange(stage_c, c_send, c_recv, CORE, turn, value)

    def start_plane(turn, value):
        return exchange(stage_p, p_send, p_recv, PLANE, turn, value)

    def start_depth(turn, value):
        return exchange(stage_d, d_send, d_recv, DEPTH, turn, value)

    def summed(copies, stage, turn):
        for copy in copies:
            copy.wait_recv()
        return jnp.sum(stage[turn], axis=0)

    def start_far(turn, copies, own):
        return start_depth(turn, unpacked(summed(copies, stage_p, turn)) + pltpu.roll(own, 3, axis=0))

    def moments_of(state):
        rows = [
            jnp.sum(blob_col[...] * state[c * PITCH : (c + 1) * PITCH, :], axis=0, keepdims=True) for c in range(3)
        ]
        return jnp.concatenate(rows + [jnp.zeros((5, BODIES), F32)], axis=0)

    def charges(moments):
        return fold(mm(stacked(moments), occupancy[...], NT))

    low_bit = lax.rem(iz, 2) == 1
    high_bit = iz // 2 == 1

    def pick(flag, a, b):
        return jnp.where(flag, a, b)

    def pair(ref):
        return (ref[0], ref[1])

    def far_values(turn, copies):
        for copy in copies:
            copy.wait_recv()
        top = iota((8, CELLS), 0) < 3
        layers = []
        for high in range(4):
            here = stage_d[turn, DEPTH.index((0, 0, 0, 0, high)) + 1 if high else 0]
            there = stage_d[turn, DEPTH.index((0, 0, 0, 1, high)) + 1]
            layers.append(jnp.where(top, here + there - pltpu.roll(here, 5, axis=0), here))
        own, one, two, three = layers
        joined = jnp.concatenate(
            [
                jnp.concatenate([pick(low_bit, one, own), pick(low_bit, own, one)], axis=1),
                jnp.concatenate([pick(low_bit, three, two), pick(low_bit, two, three)], axis=1),
            ],
            axis=0,
        )
        first = mm_few(joined, pair(up_op))
        mine, partner = first[:8], first[8:]
        second = jnp.concatenate([pick(high_bit, partner, mine), pick(high_bit, mine, partner)], axis=1)
        potential = mm_few(second, pair(root_op)) + pltpu.roll(mm_few(partner, pair(sibling_op.at[1])), 5, axis=0)
        potential = mm_few(potential, pair(down_op), NT) + pltpu.roll(mm_few(one, pair(sibling_op.at[0])), 5, axis=0)
        return jnp.where(top, fold(mm(stacked(potential), occupancy[...])), 0.0)

    def factor(target, source, inverse):
        index = 3 * source + target if inverse else 3 * target + source
        return rotation[index : index + 1, :]

    def rotated(parts, inverse):
        return [
            factor(target, 0, inverse) * parts[0] + factor(target, 1, inverse) * parts[1] + factor(target, 2, inverse) * parts[2]
            for target in range(3)
        ]

    def write_self(state, result):
        parts = [state[c * PITCH : (c + 1) * PITCH, :] for c in range(3)]
        turned = jnp.concatenate(rotated(parts, False) + [jnp.zeros((ROWS - 3 * PITCH, BODIES), F32)], axis=0)
        mixture = mm3((self_op[0], self_op[1]), split(turned))
        back = rotated([mixture[c * PITCH : (c + 1) * PITCH] for c in range(3)], True)
        for c in range(3):
            result[c * PITCH : (c + 1) * PITCH, :] = back[c]
        result[3 * PITCH :, :] = jnp.zeros((ROWS - 3 * PITCH, BODIES), F32)

    def write_own_gather(state):
        own_gather[...] = mm3((link_op[0, :, :BODIES], link_op[1, :, :BODIES]), split(state[...]), NT)

    def add_boxes(phase, first, last):
        lanes = slice(BODIES + first * RIM, BODIES + last * RIM)
        boxes = split(halo[phase, first:last].reshape((last - first) * RIM, ROWS))
        return own_gather[...] + mm3((link_op[0, :, lanes], link_op[1, :, lanes]), boxes)

    def add_far(result, values):
        for c in range(3):
            result[c * PITCH : (c + 1) * PITCH, :] += blob_col[...] * values[c : c + 1, :]

    def write_operator(source, target):
        padded_mat[...] = jnp.zeros_like(padded_mat)
        for c in range(3):
            padded_mat[c * PITCH : c * PITCH + BLOBS, : 3 * BLOBS] = source[c * BLOBS : (c + 1) * BLOBS, :]
        matrix = padded_mat[...]
        lane = iota((ROWS, ROWS), 1)
        gap = PITCH - BLOBS
        spread = jnp.where(
            lane < PITCH, matrix, jnp.where(lane < 2 * PITCH, pltpu.roll(matrix, gap, axis=1), pltpu.roll(matrix, 2 * gap, axis=1))
        )
        target[0], target[1] = split(spread)

    loads["rhs"].wait()
    for c in range(3):
        state_r[body_rows(c), :128] = rhs_in[c, :, :128]
    rim[0] = state_r[:, :128].T[:RIM]
    loads["rest"].wait()
    for c in range(3):
        state_r[body_rows(c), 128:] = rhs_in[c, :, 128:]
    loads["weight"].wait()
    loads["links"].wait()
    links = links_in[...]
    box, body = links // BODIES, lax.rem(links, BODIES)
    place = jnp.zeros_like(box)
    for slot, index in PLACES.items():
        place = jnp.where(box == slot, index, place)
    lane_of = jnp.where(box == 4, body, BODIES + place * RIM + body)
    link_rows[...] = jnp.zeros_like(link_rows)
    link_rows[0:NEIGH, :] = lane_of.astype(F32)
    link_rows[NEIGH : 2 * NEIGH, :] = weight_in[...]
    link_cols[...] = link_rows[...].T
    block = 32

    @pl.loop(0, BODIES // block)
    def _(i):
        rows = pl.ds(pl.multiple_of(i * block, block), block)
        entries = link_cols[rows, :]
        width = BODIES + NEIGH * RIM
        lane = iota((block, width), 1).astype(F32)
        weights = jnp.zeros((block, width), F32)
        for k in range(NEIGH):
            weights = weights + jnp.where(lane == entries[:, k : k + 1], entries[:, NEIGH + k : NEIGH + k + 1], 0.0)
        link_op[0, rows, :], link_op[1, rows, :] = split(weights)

    pl.semaphore_wait(barrier, len(greeted))
    start_halo(0)

    loads["blob"].wait()
    loads["cells"].wait()
    blob_row[...] = jnp.zeros_like(blob_row)
    blob_row[0:1, :BLOBS] = blob_in[...]
    diagonal = iota((PITCH, BODIES), 0) == iota((PITCH, BODIES), 1)
    blob_square = total(blob_row[0:1, :] * blob_row[0:1, :])
    column = jnp.sum(jnp.where(diagonal, blob_row[0:1, :BODIES], 0.0), axis=1, keepdims=True)
    blob_col[...] = jnp.broadcast_to(column, (PITCH, BODIES))
    occupancy[...] = jnp.where(iota((CELLS, BODIES), 0) == cells_in[...], 1.0, 0.0).astype(BF16)
    own_charges = charges(moments_of(state_r))
    copies = start_core(0, packed(own_charges))

    loads["angles"].wait()
    for target, row in enumerate(frame(angles_in[...])):
        for source, value in enumerate(row):
            rotation[3 * target + source : 3 * target + source + 1, :] = value
    copies = start_plane(0, summed(copies, stage_c, 0))
    loads["self"].wait()
    write_operator(self_in, self_op)

    for name in ("perm", "interp", "sibling", "root"):
        loads[name].wait()
    lane_few = iota((8, 512), 1)
    blob_first = blob_row[...]
    blob_rows[...] = jnp.zeros_like(blob_rows)
    for c in range(3):
        blob_rows[c : c + 1, :] = pltpu.roll(blob_first, c * PITCH, axis=1)[0:1] if c else blob_first[0:1]
    perm_row[...] = jnp.full_like(perm_row, -1.0)
    for level in range(2):
        perm = perm_in[level : level + 1, :].astype(F32)
        perm_row[level : level + 1, : 2 * SKEL] = jnp.where(perm >= SKEL, perm + (CELLS - SKEL), perm)
    perm_all = perm_row[...]
    kept_rows = jnp.where(lane_few < SKEL, perm_all, -1.0)[:, :CELLS]
    rest_rows = jnp.where(lane_few < SKEL, pltpu.roll(perm_all, 512 - SKEL, axis=1), -1.0)[:, :CELLS]
    square[...] = jnp.zeros_like(square)
    place = iota((2 * CELLS, CELLS), 0).astype(F32)
    ups = []
    for level in range(2):
        kept = jnp.where(place == kept_rows[level : level + 1], 1.0, 0.0)
        rest = jnp.where(place == rest_rows[level : level + 1], 1.0, 0.0).astype(BF16)
        square[:SKEL, :SKEL] = interp_in[level]
        high, low = split(square[...])
        ups.append(kept + (mm(rest, high) + mm(rest, low)))
        square[:SKEL, :SKEL] = sibling_in[level]
        sibling_op[level, 0], sibling_op[level, 1] = split(square[...])
    up_op[0], up_op[1] = split(ups[0])
    down_op[0], down_op[1] = split(pick(low_bit, ups[0][CELLS:], ups[0][:CELLS]))
    square[:SKEL, :SKEL] = root_in[...]
    below = mm3(split(square[...]), split(pick(high_bit, ups[1][CELLS:], ups[1][:CELLS])), NT)
    root_op[0], root_op[1] = split(mm3(split(ups[1]), split(below)))

    forward_halo(0, 2 - odd)
    copies = start_far(0, copies, own_charges)
    write_self(state_r, state_u)
    forward_halo(0, 1 + odd)

    loads["near"].wait()
    write_operator(near_in, near_op)
    write_own_gather(state_r)
    wait_boxes(0, (0, 3))
    own_gather[...] = add_boxes(0, 0, 4)
    near = pair(near_op)
    near_moments = stacked(mm_few(blob_rows[...], near))
    self_moments = moments_of(state_u)
    self_rim[...] = state_u[:, :128].T[:RIM]
    values = far_values(0, copies)
    columns = jnp.concatenate([values, jnp.zeros((120, BODIES), F32)], axis=0)[:, :128].T[:RIM]
    self_rim[...] += sum(columns[:, c : c + 1] * blob_rows[c : c + 1, :] for c in range(3))
    add_far(state_u, values)
    drain()
    wait_boxes(0, (4, 5, 6, 7))

    high, low = split(add_boxes(0, 4, 8))
    moments = self_moments + blob_square * values + fold(mm(near_moments, high, NT) + mm(near_moments, low, NT))
    own_charges = charges(moments)
    copies = start_core(1, packed(own_charges))
    rim[1] = self_rim[...] + mm3((high[:RIM], low[:RIM]), near, NT)
    start_halo(1)
    state_u[...] += mm3(near, (high, low), NT)
    copies = start_plane(1, summed(copies, stage_c, 1))
    write_self(state_u, state_t)
    write_own_gather(state_u)
    forward_halo(1, 2 - odd)
    for c in range(3):
        u_out[c] = state_u[body_rows(c), :]

    tiny = 1e-30
    rr = total(state_r[...] * state_r[...])
    ru = total(state_r[...] * state_u[...])
    over_rr = jnp.where(rr > 0.0, 1.0 / jnp.where(rr > 0.0, rr, 1.0), 0.0)
    copies = start_far(1, copies, own_charges)
    forward_halo(1, 1 + odd)
    state_u[...] = state_u[...] - (ru * over_rr) * state_r[...]
    uu = total(state_u[...] * state_u[...])
    over_uu = jnp.where(uu > 0.0, 1.0 / jnp.where(uu > 0.0, uu, 1.0), 0.0)
    wait_boxes(1, (0, 3))
    own_gather[...] = add_boxes(1, 0, 4)
    drain()

    add_far(state_t, far_values(1, copies))
    wait_boxes(1, (4, 5, 6, 7))
    state_t[...] += mm3(near, split(add_boxes(1, 4, 8)), NT)

    largest = jnp.maximum(jnp.max(jnp.abs(state_t[...]), axis=(0, 1), keepdims=True), tiny)
    scaled = state_t[...] * (1.0 / largest)
    state_t[...] = scaled
    rt = total(state_r[...] * scaled)
    ut = total(state_u[...] * scaled)
    state_t[...] = state_t[...] - (rt * over_rr) * state_r[...] - (ut * over_uu) * state_u[...]
    tt = total(state_t[...] * state_t[...])
    root_rr, root_uu = jnp.sqrt(rr), jnp.sqrt(uu)
    triangle = [
        root_rr,
        ru * over_rr * root_rr,
        root_uu,
        largest * (rt * over_rr * root_rr),
        largest * (ut * over_uu * root_uu),
        largest * jnp.sqrt(tt),
    ]
    height = 2 * iz + odd
    row_of = iota((8, 128), 0)
    lane_is_mine = iota((8, 128), 1) == 4 * ix + iy // 2 + 32 * lax.rem(height, 4)
    tile = jnp.zeros((8, 128), F32)
    for i, value in enumerate(triangle):
        tile = jnp.where((row_of == i) & lane_is_mine, value, tile)
    copies = start_core(2, tile)
    copies = start_plane(2, summed(copies, stage_c, 2))
    tile = summed(copies, stage_p, 2)
    copies = start_depth(2, jnp.concatenate([jnp.where(height < 4, tile, 0.0), jnp.where(height < 4, 0.0, tile)], axis=1))
    drain()
    everyone = summed(copies, stage_d, 2)

    r1, u1, u2, t1, t2, t3 = (everyone[i : i + 1] for i in range(6))
    dot = lambda *pairs: total(sum(a * b for a, b in pairs))
    beta = jnp.sqrt(dot((r1, r1)) + epsilon)
    v1 = r1 / beta
    image1, image2 = v1 + u1 / beta, u2 / beta
    diag_first = dot((image1, v1))
    w1, w2 = image1 - diag_first * v1, image2
    below_first = jnp.sqrt(dot((w1, w1), (w2, w2)) + epsilon)
    second1, second2 = w1 / below_first, w2 / below_first
    rest = (1.0 - diag_first) / beta
    z1 = second1 + (t1 / beta + rest * u1) / below_first
    z2 = second2 + (t2 / beta + rest * u2) / below_first
    z3 = (t3 / beta) / below_first
    above_second = dot((z1, v1))
    diag_second = dot((z1, second1), (z2, second2))
    left1 = z1 - above_second * v1 - diag_second * second1
    left2 = z2 - diag_second * second2
    below_second = jnp.sqrt(dot((left1, left1), (left2, left2), (z3, z3)) + epsilon)
    coef_one, coef_two, residual = least_squares(beta, diag_first, below_first, above_second, diag_second, below_second)
    on_r = coef_one / beta + coef_two * rest / below_first
    on_u = coef_two / (below_first * beta)
    for c in range(3):
        u_out[c] = on_r * rhs_in[c] + on_u * u_out[c]
    store = pltpu.make_async_copy(u_out, result_hbm.at[:, :, 0, :], out_sem)
    store.start()
    residual_ref[...] = residual

    store.wait()


def body(rhs, angles, self_mob, near_mat, near_weight, neighbours, cells, blob_weight, skel_perm, interp, sibling_ops, root_op):
    initial = rhs.reshape(3, BLOBS, 1, BODIES)
    operands = [
        initial,
        angles.reshape(3, 1, BODIES),
        self_mob,
        near_mat,
        near_weight.reshape(NEIGH, BODIES),
        neighbours.reshape(NEIGH, BODIES),
        cells.reshape(1, BODIES),
        blob_weight.reshape(1, BLOBS),
        skel_perm,
        interp,
        sibling_ops,
        root_op,
    ]
    vmem = pltpu.VMEM
    dma = pltpu.SemaphoreType.DMA
    result, residual = pl.pallas_call(
        kernel,
        out_shape=(
            jax.ShapeDtypeStruct(initial.shape, F32),
            jax.ShapeDtypeStruct((1, 1), F32),
        ),
        in_specs=[pl.BlockSpec(memory_space=pltpu.HBM)] * len(operands),
        out_specs=(
            pl.BlockSpec(memory_space=pltpu.HBM),
            pl.BlockSpec(memory_space=pltpu.VMEM),
        ),
        scratch_shapes=[vmem((3, BLOBS, BODIES), F32), vmem((3, BODIES), F32)]
        + [vmem(x.shape, x.dtype) for x in operands[2:]]
        + [
            vmem((ROWS, BODIES), F32),
            vmem((ROWS, BODIES), F32),
            vmem((ROWS, BODIES), F32),
            vmem((ROWS, ROWS), F32),
            vmem((2, ROWS, ROWS), BF16),
            vmem((2, ROWS, ROWS), BF16),
            vmem((2, BODIES, BODIES + NEIGH * RIM), BF16),
            vmem((BODIES, 128), F32),
            vmem((128, BODIES), F32),
            vmem((CELLS, BODIES), BF16),
            vmem((8, ROWS), F32),
            vmem((8, ROWS), F32),
            vmem((PITCH, BODIES), F32),
            vmem((16, BODIES), F32),
            vmem((8, 512), F32),
            vmem((CELLS, CELLS), F32),
            vmem((2, 2 * CELLS, CELLS), BF16),
            vmem((2, CELLS, CELLS), BF16),
            vmem((2, 2, CELLS, CELLS), BF16),
            vmem((2, 2 * CELLS, CELLS), BF16),
            vmem((BODIES, ROWS), F32),
            vmem((RIM, ROWS), F32),
            vmem((3, BLOBS, BODIES), F32),
            vmem((2, RIM, ROWS), F32),
            vmem((2, NEIGH, RIM, ROWS), F32),
            vmem((3, len(CORE) + 1, 8, 128), F32),
            vmem((3, len(PLANE) + 1, 8, 128), F32),
            vmem((3, len(DEPTH) + 1, 8, 256), F32),
            dma((len(operands) + 1,)),
            dma(()),
            dma((2, NEIGH, PARTS)),
            dma((2, NEIGH, PARTS)),
            dma((3, len(CORE))),
            dma((3, len(CORE))),
            dma((3, len(PLANE))),
            dma((3, len(PLANE))),
            dma((3, len(DEPTH))),
            dma((3, len(DEPTH))),
        ],
        compiler_params=pltpu.CompilerParams(collective_id=0, has_side_effects=True, vmem_limit_bytes=64 * 2**20),
    )(*operands)
    return (result.reshape(rhs.shape), residual.reshape(()))


def solution(mesh):
    in_specs = (
        P("gx", "gy", None, None, "gz"),
        P("gx", "gy", None, "gz"),
        P(),
        P(),
        P("gx", "gy", None, "gz"),
        P("gx", "gy", None, "gz"),
        P("gx", "gy", "gz"),
        P(),
        P(),
        P(),
        P(),
        P(),
    )
    out_specs = (P("gx", "gy", None, None, "gz"), P())
    return jax.shard_map(body, mesh=mesh, in_specs=in_specs, out_specs=out_specs, check_vma=False)
```
